512 devices in a mesh: grow: 16 (over y, core), gcol: 32 (over x, z).
Axes of the slice: x: 4, y: 8, z: 8, core: 2. Of those that a mesh axis runs over, the one named last changes fastest.
Arguments:
- pair_density: bfloat16 [16384, 2048], P('gcol', 'grow'), may hold values from -0.125 to 0.125
- pair_weight: float32 [2048], P('grow'), may hold values from 0.25 to 4
- coulomb: float32 [16384], replicated, may hold values from 0.25 to 4
- pivot_rows: int32 [512], replicated, may hold values from 0 to 16383, as said below
Outputs:
- dielectric: float32 [16384, 16384], P('grow', 'gcol')
- panel_factor: float32 [16384, 512], P('grow')
The draws below stay inside these ranges and needn't reach their ends.
Inputs may be any that keep to these rules, and one draw needn't show every extreme that they name: `pivot_rows`: 512 distinct plane-wave indices, exactly one in each run of 32 consecutive plane waves starting at a multiple of it; 0 and 16383 are always among them.
All inputs are finite; a program needn't handle non-finite values.
Results may differ from the reference program's by a relative error of at most 0.0038.
Values may be sent and summed in bfloat16 or wider, within the bound.
A program may use at most 64 MiB of HBM per device.

```python
import math
import jax
import jax.numpy as jnp
from jax import lax

NG = 16384
PAIRS = 2048
PANEL = 512


def draw_pivot_rows(key, part):
    stride = NG // PANEL
    within = jax.random.randint(key, (PANEL,), 0, stride).astype(jnp.int32)
    slots = lax.iota(jnp.int32, PANEL)
    within = jnp.where(slots == 0, 0, within).astype(jnp.int32)
    within = jnp.where(slots == PANEL - 1, stride - 1, within).astype(jnp.int32)
    picked = (slots * stride + within).astype(jnp.int32)
    order = jax.random.permutation(jax.random.fold_in(key, 7), PANEL)
    return picked[order].astype(jnp.int32)


def level_of(own_key, extent, split, smallest, top_value):
    loudness = 1.0
    for dim, parts in split:
        steps = jax.random.uniform(jax.random.fold_in(jax.random.fold_in(own_key, 6), dim), (parts,), jnp.float32, smallest / len(split), top_value / len(split))
        loudness = loudness * jnp.repeat(jnp.exp(steps), extent[dim] // parts).reshape((-1,) + (1,) * (len(extent) - 1 - dim))
    return loudness


def scatter_about(own_key, shape, scale, reach, shards=(), dtype=jnp.bfloat16):
    values = jax.random.normal(own_key, shape, jnp.float32) * scale
    if len(shards) > 0:
        values = level_of(own_key, shape, shards, -0.22, 0.18) * values
    return jnp.clip(values, min=-reach, max=reach).astype(dtype)


def setup_inputs(seed: int = 0) -> dict:
    key_list = jax.random.split(jax.random.key(seed), 5)
    return {
        "pair_density": scatter_about(key_list[0], (NG, PAIRS), PAIRS ** -0.5, 0.125, ((0, 32), (1, 16))),
        "pair_weight": jnp.clip(jnp.exp(math.log(4.0) - 2.7725887 * jax.random.uniform(key_list[1], (PAIRS,), jnp.float32) ** level_of(key_list[1], (PAIRS,), ((0, 16),), -0.2, 0.2)), 0.25, 4.0),
        "coulomb": jnp.clip(jnp.exp(jax.random.uniform(key_list[2], (NG,), jnp.float32, math.log(0.25), math.log(4.0))), 0.25, 4.0),
        "pivot_rows": draw_pivot_rows(jax.random.fold_in(key_list[4], 71), 0),
    }


def factor_rows(columns_in, row_numbers, pivot_block, pivot_rows):
    width = pivot_rows.shape[0]
    factor = jnp.linalg.cholesky(pivot_block)
    pivot_diag = jnp.diagonal(factor)
    solved = lax.linalg.triangular_solve(factor, columns_in, left_side=False, lower=True, transpose_a=True)
    lower_part = solved / pivot_diag[None, :]
    upper = pivot_diag[:, None] * factor.T
    column_iota = lax.iota(jnp.int32, width)
    matches = row_numbers[:, None] == pivot_rows[None, :]
    is_pivot = jnp.any(matches, axis=1)
    position = lax.optimization_barrier(jnp.sum(jnp.where(matches, column_iota[None, :], 0), axis=1)).astype(jnp.int32)
    top_rows = jnp.take(upper, position, axis=0)
    upper_mask = is_pivot[:, None] & (column_iota[None, :] >= position[:, None])
    return jnp.where(upper_mask, top_rows, lower_part)

def reference(pair_density, pair_weight, coulomb, pivot_rows):
    scaled = (pair_density.astype(jnp.float32) * jnp.sqrt(pair_weight)[None, :]).astype(jnp.bfloat16)
    gram_full = jnp.dot(scaled.astype(jnp.float32), scaled.T.astype(jnp.float32), preferred_element_type=jnp.float32)
    root_kernel = jnp.sqrt(coulomb)
    indices = lax.iota(jnp.int32, NG)
    identity = jnp.where(indices[:, None] == indices[None, :], 1.0, 0.0).astype(jnp.float32)
    dielectric = root_kernel[:, None] * root_kernel[None, :] * gram_full + identity
    columns = jnp.take(dielectric, pivot_rows, axis=1)
    pivot_block = jnp.take(columns, pivot_rows, axis=0)
    panel_factor = factor_rows(columns, indices, pivot_block, pivot_rows)
    return (dielectric, panel_factor)
```

```python
import functools

import jax
import jax.numpy as jnp
from jax import lax
from jax.experimental import pallas as pl
from jax.experimental.pallas import tpu as pltpu
from jax.sharding import Mesh
from jax.sharding import PartitionSpec as P

NG = 16384
PANEL = 512
RUN = NG // PANEL
NY, NC, NX, NZ = 8, 2, 4, 8
COLS = NG // (NX * NZ)
ROWS = NG // (NY * NC)
OWN = 128
HALF = NY * OWN
MINE = COLS // RUN
HI = lax.Precision.HIGHEST
f32, bf16 = jnp.float32, jnp.bfloat16
MESH_ID = pl.DeviceIdType.MESH


def iota(shape, dim):
    return lax.broadcasted_iota(jnp.int32, shape, dim)


def eye(n):
    return iota((n, n), 0) == iota((n, n), 1)


def column_of(row):
    blocks = []
    for i in range(row.shape[1] // 128):
        part = jnp.broadcast_to(row[:, i * 128 : (i + 1) * 128], (128, 128))
        blocks.append(jnp.sum(jnp.where(eye(128), part, 0.0), axis=1, keepdims=True))
    return jnp.concatenate(blocks, axis=0)


def row_of(column):
    blocks = []
    for i in range(column.shape[0] // 128):
        part = jnp.broadcast_to(column[i * 128 : (i + 1) * 128], (128, 128))
        blocks.append(jnp.sum(jnp.where(eye(128), part, 0.0), axis=0, keepdims=True))
    return jnp.concatenate(blocks, axis=1)


def lanes_of(ref, first, count):
    return jnp.concatenate([ref[pl.ds(first + i, 1), :] for i in range(count)], axis=1)


def times_t(a, b, precision=None):
    return lax.dot_general(
        a, b, (((1,), (1,)), ((), ())), precision=precision, preferred_element_type=f32
    )


def t_times(a, b, precision=None):
    return lax.dot_general(
        a, b, (((0,), (0,)), ((), ())), precision=precision, preferred_element_type=f32
    )


def split3(y):
    high = y.astype(bf16).astype(f32)
    rest = y - high
    middle = rest.astype(bf16).astype(f32)
    return high, middle, rest - middle


def eight_rows(s_ref, c):
    sub = iota((8, 128), 0)
    rows = s_ref[c : c + 8, :]
    cols = [jnp.broadcast_to(rows[:, c + j : c + j + 1], (8, 128)) for j in range(8)]
    left, right = rows[:, :128], rows[:, 128:]
    for j in range(8):
        r = lax.rsqrt(jnp.broadcast_to(cols[j][j : j + 1, :], (8, 128)))
        f = jnp.where(sub > j, cols[j] * r, 0.0)
        own = jnp.where(sub == j, r, 1.0)
        for m in range(j + 1, 8):
            cols[m] = cols[m] - f * (jnp.broadcast_to(cols[m][j : j + 1, :], (8, 128)) * r)
        left_j = jnp.broadcast_to(left[j : j + 1, :], (8, 128)) * r
        right_j = jnp.broadcast_to(right[j : j + 1, :], (8, 128)) * r
        left = left * own - f * left_j
        right = right * own - f * right_j
    y = jnp.concatenate([left, right], axis=1)
    s_ref[c : c + 8, :] = y
    if c + 8 < 128:
        h, m, l = split3(y)
        lhs = jnp.concatenate([h, h, m, h, l, m], axis=0)[:, :128].astype(bf16)
        rhs = jnp.concatenate([h, m, h, l, h, m], axis=0).astype(bf16)
        s_ref[c + 8 :, :] = s_ref[c + 8 :, :] - t_times(lhs, rhs)[c + 8 :, :]


def factor_and_inverse(aug, s_ref, between):
    def block(k, carry):
        o = pl.multiple_of(k * 128, 128)
        s_ref[:, :128] = aug[pl.ds(o, 128), pl.ds(o, 128)]
        s_ref[:, 128:] = eye(128).astype(f32)
        for b in range(16):
            eight_rows(s_ref, 8 * b)
            between(k, b)
        aug[pl.ds(o, 128), :] = jnp.dot(
            s_ref[:, 128:], aug[pl.ds(o, 128), :], precision=HI, preferred_element_type=f32
        )
        for i in range(1, 4):

            @pl.when(i > k)
            def _():
                lhs = aug[pl.ds(o, 128), i * 128 : (i + 1) * 128]
                update = t_times(lhs, aug[pl.ds(o, 128), :], HI)
                aug[i * 128 : (i + 1) * 128, :] = aug[i * 128 : (i + 1) * 128, :] - update

        return carry

    lax.fori_loop(0, 4, block, 0)


def prologue(density_ref, weight_ref, pivots_ref, scaled_ref, picked_ref):
    first = (lax.axis_index("x") * NZ + lax.axis_index("z")) * COLS
    scaled = (density_ref[...].astype(f32) * jnp.sqrt(weight_ref[...])).astype(bf16)
    scaled_ref[...] = scaled
    pivots = column_of(jnp.concatenate([pivots_ref[i : i + 1, :] for i in range(4)], axis=1).astype(f32))
    waves = (first + iota((PANEL, COLS), 1)).astype(f32)
    taken = jnp.sum(jnp.where(pivots == waves, 1.0, 0.0), axis=0, keepdims=True)
    in_run = iota((MINE, COLS), 1) // RUN == iota((MINE, COLS), 0)
    one_hot = jnp.where(in_run, jnp.broadcast_to(taken, (MINE, COLS)), 0.0).astype(bf16)
    picked_ref[...] = jnp.dot(one_hot, scaled, preferred_element_type=f32).astype(bf16)


class Gather:
    def __init__(self, slot, line, sems, place):
        self.slot, self.line, self.sems, self.place = slot, line, sems, place

    def ring_z(self, view, step, base):
        y, c, x, z = self.place
        send, recv = self.sems
        out = []
        right, left = lax.rem(z + 1, NZ), lax.rem(z + NZ - 1, NZ)
        from_left = lax.rem(z + NZ - step + 1, NZ), lax.rem(z + NZ - step, NZ)
        k = base + 2 * (step - 1)
        out.append((view(from_left[0]), view(from_left[1]), k, (y, c, x, right)))
        if step < 4:
            from_right = lax.rem(z + step - 1, NZ), lax.rem(z + step, NZ)
            out.append((view(from_right[0]), view(from_right[1]), k + 1, (y, c, x, left)))
        return out

    def ring_x(self, view, half, step, base):
        y, c, x, z = self.place
        right, left = lax.rem(x + 1, NX), lax.rem(x + NX - 1, NX)
        opposite = lax.rem(x + 2, NX)
        k = base + 2 * (step - 1)
        if step == 1:
            return [
                (view(x), view(left), k, (y, c, right, z)),
                (view(x), view(right), k + 1, (y, c, left, z)),
            ]
        return [
            (half(left, 0), half(opposite, 0), k, (y, c, right, z)),
            (half(right, 1), half(opposite, 1), k + 1, (y, c, left, z)),
        ]

    def copies(self, core, step):
        x, z = self.place[2], self.place[3]
        if core == 0:
            if step < 4:
                return self.ring_z(lambda i: self.slot(x, i), step + 1, 0)
            return self.ring_x(
                lambda i: self.line(0, i), lambda i, h: self.line(0, i, h), step - 3, 7
            )
        if step < 2:
            return self.ring_x(
                lambda i: self.slot(i, z), lambda i, h: self.slot(i, z, h), step + 1, 7
            )
        return self.ring_z(lambda i: self.line(1, i), step - 1, 0)

    def each(self, core, step, do):
        send, recv = self.sems
        for sent, received, k, device in self.copies(core, step):
            do(sent, received, send.at[k], recv.at[k], device)

    def start(self, core, step):
        def go(sent, received, s, r, device):
            pltpu.make_async_remote_copy(sent, sent, s, r, device, MESH_ID).start()

        self.each(core, step, go)

    def wait_recv(self, core, step):
        def go(sent, received, s, r, device):
            pltpu.make_async_remote_copy(received, received, s, r, device, MESH_ID).wait_recv()

        self.each(core, step, go)

    def wait_send(self, core, step):
        def go(sent, received, s, r, device):
            pltpu.make_async_remote_copy(sent, sent, s, r, device, MESH_ID).wait_send()

        self.each(core, step, go)

    def advance(self, event):
        for core in range(2):

            @pl.when(self.place[1] == core)
            def _():
                if event > 0:
                    self.wait_recv(core, event - 1)
                if event < 6:
                    self.start(core, event)

    def drain(self):
        for core in range(2):

            @pl.when(self.place[1] == core)
            def _():
                for step in range(6):
                    self.wait_send(core, step)


def main_kernel(
    scaled_ref,
    picked_ref,
    coulomb_ref,
    pivots_ref,
    dielectric_ref,
    panel_ref,
    q_ref,
    r_ref,
    c_ref,
    qp_ref,
    aug,
    s_ref,
    columns_ref,
    local_sem,
    qy_send,
    qy_recv,
    qg_send,
    qg_recv,
    rg_send,
    rg_recv,
    cy_send,
    cy_recv,
    one_send,
    one_recv,
):
    y, c, x, z = (lax.axis_index(a) for a in ("y", "c", "x", "z"))
    place = (y, c, x, z)
    partner = (y, 1 - c, x, z)

    def shift(plane, core):
        return lax.rem(plane + 12 - 4 * lax.rem(plane, 2) - 2 * core, NY)

    to_y, to_c = 2 * x + z // 4, lax.rem(z // 2, 2)
    to_half = lax.rem(z, 2)
    target = (to_y, to_c, 2 * to_half + c, lax.rem(y + NZ - shift(to_y, to_c), NZ))
    mine = shift(y, c)

    def owner_of(zz):
        return lax.rem(zz + mine, NY)

    origin = (owner_of(z), lax.rem(x, 2), y // 2, 4 * lax.rem(y, 2) + 2 * c + x // 2)

    def r_block(pair_core, half, owner):
        return r_ref.at[
            pair_core,
            pl.ds(pl.multiple_of(half * COLS, COLS), COLS),
            pl.ds(pl.multiple_of(owner * OWN, OWN), OWN),
        ]

    def r_slot(xx, zz, part=None):
        first, count = (xx // 2) * COLS, COLS
        if part is not None:
            first, count = first + part * (COLS // 2), COLS // 2
        return r_ref.at[
            lax.rem(xx, 2),
            pl.ds(pl.multiple_of(first, 256), count),
            pl.ds(pl.multiple_of(owner_of(zz) * OWN, OWN), OWN),
        ]

    def r_line(core, i, part=None):
        if core == 0:
            first, count = (i // 2) * COLS, COLS
            if part is not None:
                first, count = first + part * (COLS // 2), COLS // 2
            return r_ref.at[lax.rem(i, 2), pl.ds(pl.multiple_of(first, 256), count), :]
        return r_ref.at[:, :, pl.ds(pl.multiple_of(owner_of(i) * OWN, OWN), OWN)]

    def q_slot(xx, zz, part=None):
        rows = pl.ds(pl.multiple_of(zz * MINE, MINE), MINE)
        cols = slice(None) if part is None else pl.ds(part * (HALF // 2), HALF // 2)
        return q_ref.at[c, xx, rows, cols]

    def q_line(core, i, part=None):
        if core == 0:
            rows = slice(None) if part is None else pl.ds(part * 64, 64)
            return q_ref.at[c, i, rows, :]
        return q_ref.at[c, :, pl.ds(pl.multiple_of(i * MINE, MINE), MINE), :]

    q_gather = Gather(q_slot, q_line, (qg_send, qg_recv), place)
    r_gather = Gather(r_slot, r_line, (rg_send, rg_recv), place)

    barrier = pltpu.get_barrier_semaphore()
    greeted = [(lax.rem(y + d, NY), c, x, z) for d in range(1, NY)]
    greeted += [(y, c, x, lax.rem(z + d, NZ)) for d in (1, NZ - 1)]
    greeted += [(y, c, lax.rem(x + d, NX), z) for d in (1, NX - 1)]
    greeted += [partner, target, origin]
    for device in greeted:
        pl.semaphore_signal(barrier, 1, device_id=device, device_id_type=MESH_ID)

    own_q = q_ref.at[c, x, pl.ds(pl.multiple_of(z * MINE, MINE), MINE), pl.ds(pl.multiple_of(y * OWN, OWN), OWN)]
    own_c = c_ref.at[c, :, pl.ds(pl.multiple_of(y * OWN, OWN), OWN)]
    keep_q = pltpu.make_async_copy(picked_ref, own_q, local_sem.at[0])
    keep_c = pltpu.make_async_copy(scaled_ref, own_c, local_sem.at[1])
    keep_q.start()
    keep_c.start()
    pl.semaphore_wait(barrier, len(greeted))

    def picked_copy(d):
        peer = (lax.rem(y + d, NY), c, x, z)
        return pltpu.make_async_remote_copy(
            picked_ref, own_q, qy_send.at[d], qy_recv.at[d], peer, MESH_ID
        )

    def picked_arrival(d):
        other = lax.rem(y + NY - d, NY)
        there = q_ref.at[c, x, pl.ds(pl.multiple_of(z * MINE, MINE), MINE), pl.ds(pl.multiple_of(other * OWN, OWN), OWN)]
        return pltpu.make_async_remote_copy(
            there, there, qy_send.at[d], qy_recv.at[d], partner, MESH_ID
        )

    for d in (4, 3, 5, 2, 6, 1, 7):
        picked_copy(d).start()

    spread = pltpu.make_async_remote_copy(
        scaled_ref, r_block(c, to_half, y), one_send.at[0], one_recv.at[0], target, MESH_ID
    )
    arrived = r_slot(x, z)
    spread_in = pltpu.make_async_remote_copy(
        arrived, arrived, one_send.at[0], one_recv.at[0], origin, MESH_ID
    )

    def c_of(owner):
        return c_ref.at[c, :, pl.ds(pl.multiple_of(owner * OWN, OWN), OWN)]

    def ring_y(step):
        up, down = (lax.rem(y + 1, NY), c, x, z), (lax.rem(y + NY - 1, NY), c, x, z)
        k = 2 * (step - 1)
        out = [(c_of(lax.rem(y + NY - step + 1, NY)), c_of(lax.rem(y + NY - step, NY)), k, up)]
        if step < 4:
            out.append((c_of(lax.rem(y + step - 1, NY)), c_of(lax.rem(y + step, NY)), k + 1, down))
        return out

    def c_copies(step, received):
        for sent, came, k, device in ring_y(step):
            ref = came if received else sent
            yield pltpu.make_async_remote_copy(ref, ref, cy_send.at[k], cy_recv.at[k], device, MESH_ID)

    def half_of(ref, k):
        ours, theirs = ref.at[c], ref.at[1 - c]
        out = pltpu.make_async_remote_copy(ours, ours, one_send.at[k], one_recv.at[k], partner, MESH_ID)
        back = pltpu.make_async_remote_copy(theirs, theirs, one_send.at[k], one_recv.at[k], partner, MESH_ID)
        return out, back

    q_out, q_back = half_of(q_ref, 1)
    c_out, c_back = half_of(c_ref, 2)

    def c_advance(event):
        if event > 1:
            for copy in c_copies(event - 1, True):
                copy.wait_recv()
        if event < 5:
            for copy in c_copies(event, False):
                copy.start()
        if event == 5:
            c_out.start()

    keep_q.wait()
    for d in range(1, NY):
        picked_arrival(d).wait_recv()
    q_gather.advance(0)
    spread.start()
    keep_c.wait()
    c_advance(1)

    pivot_row = jnp.concatenate([pivots_ref[i : i + 1, :] for i in range(4)], axis=1)
    run_column = column_of((pivot_row // RUN).astype(f32))
    high_column = column_of((pivot_row // 128).astype(f32))
    low_column = column_of((pivot_row % 128).astype(f32))
    in_row = (high_column == iota((PANEL, 128), 1).astype(f32)).astype(f32)
    picked = jnp.dot(in_row, coulomb_ref[...], precision=HI, preferred_element_type=f32)
    at_lane = low_column == iota((PANEL, 128), 1).astype(f32)
    pivot_scale = jnp.sqrt(jnp.sum(jnp.where(at_lane, picked, 0.0), axis=1, keepdims=True))
    pivot_scale_row = row_of(pivot_scale)
    order = (run_column == iota((PANEL, PANEL), 1).astype(f32)).astype(bf16)

    for event in range(1, 7):
        q_gather.advance(event)
        if event == 3:
            c_advance(2)
    q_out.start()
    q_back.wait_recv()

    gram = None
    for h in range(2):
        qp_ref[h] = jnp.dot(
            order, q_ref[h].reshape(PANEL, HALF), preferred_element_type=f32
        ).astype(bf16)
        part = times_t(qp_ref[h], qp_ref[h])
        gram = part if gram is None else gram + part
    unit = eye(PANEL).astype(f32)
    aug[:, :PANEL] = pivot_scale * pivot_scale_row * gram + unit
    aug[:, PANEL:] = unit

    def between(k, b):
        def at(block, event):
            @pl.when(k == block)
            def _():
                event()

        if b == 0:

            @pl.when(k == 0)
            def _():
                spread_in.wait_recv()

            at(0, lambda: r_gather.advance(0))
            at(1, lambda: r_gather.advance(2))
            at(2, lambda: r_gather.advance(4))
            at(0, lambda: c_advance(3))
            at(1, lambda: c_advance(5))
        if b == 8:
            at(0, lambda: r_gather.advance(1))
            at(1, lambda: r_gather.advance(3))
            at(2, lambda: r_gather.advance(5))
            at(0, lambda: c_advance(4))

    factor_and_inverse(aug, s_ref, between)

    lt = aug[:, :PANEL]
    row_i, col_i = iota((PANEL, PANEL), 0), iota((PANEL, PANEL), 1)
    diag = jnp.sum(jnp.where(row_i == col_i, lt, 0.0), axis=1, keepdims=True)
    upper = jnp.where(col_i >= row_i, lt * diag, 0.0)
    aug[:, PANEL:] = aug[:, PANEL:] / diag

    c_back.wait_recv()
    r_gather.advance(6)

    first_row = (y * NC + c) * ROWS
    first_col = (x * NZ + z) * COLS
    row_scale = jnp.sqrt(column_of(lanes_of(coulomb_ref, (y * NC + c) * 8, 8)))
    col_scale = jnp.sqrt(lanes_of(coulomb_ref, (x * NZ + z) * 4, 4))
    tile = 256
    for t in range(ROWS // tile):
        rows = slice(t * tile, (t + 1) * tile)
        scale = row_scale[rows]
        numbers = first_row + t * tile + iota((tile, COLS), 0)
        gram = times_t(r_ref[0, rows, :], c_ref[0]) + times_t(r_ref[1, rows, :], c_ref[1])
        same = numbers == first_col + iota((tile, COLS), 1)
        dielectric_ref[rows, :] = scale * col_scale * gram + jnp.where(same, 1.0, 0.0)
        gram = times_t(r_ref[0, rows, :], qp_ref[0]) + times_t(r_ref[1, rows, :], qp_ref[1])
        same = numbers == pivot_row
        columns_ref[...] = scale * pivot_scale_row * gram + jnp.where(same, 1.0, 0.0)
        panel_ref[rows, :256] = times_t(columns_ref[:, :256], aug[:256, PANEL : PANEL + 256], HI)
        panel_ref[rows, 256:] = times_t(columns_ref[...], aug[256:, PANEL:], HI)

    runs = ROWS // RUN
    run_row = pivot_row // RUN
    mine_here = run_row == (y * NC + c) * runs + iota((runs, PANEL), 0)
    pick = mine_here.astype(f32)
    top = jnp.dot(pick, upper, precision=HI, preferred_element_type=f32)
    position = jnp.sum(pick * iota((runs, PANEL), 1).astype(f32), axis=1, keepdims=True)
    within = jnp.sum(pick * jnp.broadcast_to((pivot_row % RUN).astype(f32), (runs, PANEL)), axis=1, keepdims=True)
    lane = iota((RUN, PANEL), 1).astype(f32)
    line = iota((RUN, PANEL), 0).astype(f32)
    for q in range(runs):
        rows = slice(q * RUN, (q + 1) * RUN)
        over = (line == within[q : q + 1]) & (lane >= position[q : q + 1])
        panel_ref[rows, :] = jnp.where(over, jnp.broadcast_to(top[q : q + 1, :], (RUN, PANEL)), panel_ref[rows, :])

    for d in range(1, NY):
        picked_copy(d).wait_send()
    spread.wait_send()
    for step in range(1, 5):
        for copy in c_copies(step, False):
            copy.wait_send()
    q_out.wait_send()
    c_out.wait_send()
    q_gather.drain()
    r_gather.drain()


def body(pair_density, pair_weight, coulomb, pivot_rows):
    vmem = pl.BlockSpec(memory_space=pltpu.VMEM)
    pivots = pivot_rows.reshape(4, 128)
    scaled, picked = pl.pallas_call(
        prologue,
        out_shape=(
            jax.ShapeDtypeStruct((COLS, OWN), bf16),
            jax.ShapeDtypeStruct((MINE, OWN), bf16),
        ),
        in_specs=[vmem] * 3,
        out_specs=(vmem, vmem),
        name="scale_and_pick",
    )(pair_density, pair_weight.reshape(1, OWN), pivots)
    dma = pltpu.SemaphoreType.DMA
    return pl.pallas_call(
        main_kernel,
        out_shape=(
            jax.ShapeDtypeStruct((ROWS, COLS), f32),
            jax.ShapeDtypeStruct((ROWS, PANEL), f32),
        ),
        in_specs=[vmem] * 4,
        out_specs=(vmem, vmem),
        scratch_shapes=[
            pltpu.VMEM((2, NX, NZ * MINE, HALF), bf16),
            pltpu.VMEM((2, ROWS, HALF), bf16),
            pltpu.VMEM((2, COLS, HALF), bf16),
            pltpu.VMEM((2, PANEL, HALF), bf16),
            pltpu.VMEM((PANEL, 2 * PANEL), f32),
            pltpu.VMEM((128, 256), f32),
            pltpu.VMEM((256, PANEL), f32),
            dma((2,)),
            dma((NY,)),
            dma((NY,)),
            dma((11,)),
            dma((11,)),
            dma((11,)),
            dma((11,)),
            dma((7,)),
            dma((7,)),
            dma((3,)),
            dma((3,)),
        ],
        compiler_params=pltpu.CompilerParams(
            collective_id=0, has_side_effects=True, vmem_limit_bytes=60 * 2**20
        ),
        name="gather_factor_panel",
    )(scaled, picked, coulomb.reshape(128, 128), pivots)


def solution(mesh):
    finer = Mesh(mesh.devices.reshape(NY, NC, NX, NZ), ("y", "c", "x", "z"))
    return jax.shard_map(
        body,
        mesh=finer,
        in_specs=(P(("x", "z"), ("y", "c")), P(("y", "c")), P(), P()),
        out_specs=(P(("y", "c"), ("x", "z")), P(("y", "c"), None)),
        check_vma=False,
    )
```

```python
import functools

import jax
import jax.numpy as jnp
from jax import lax
from jax.experimental import pallas as pl
from jax.experimental.pallas import tpu as pltpu
from jax.sharding import Mesh
from jax.sharding import PartitionSpec as P

NG = 16384
PANEL = 512
RUN = NG // PANEL
NY, NC, NX, NZ = 8, 2, 4, 8
COLS = NG // (NX * NZ)
ROWS = NG // (NY * NC)
OWN = 128
HALF = NY * OWN
MINE = COLS // RUN
HI = lax.Precision.HIGHEST
f32, bf16 = jnp.float32, jnp.bfloat16
MESH_ID = pl.DeviceIdType.MESH


def iota(shape, dim):
    return lax.broadcasted_iota(jnp.int32, shape, dim)


def eye(n):
    return iota((n, n), 0) == iota((n, n), 1)


def column_of(row):
    blocks = []
    for i in range(row.shape[1] // 128):
        part = jnp.broadcast_to(row[:, i * 128 : (i + 1) * 128], (128, 128))
        blocks.append(jnp.sum(jnp.where(eye(128), part, 0.0), axis=1, keepdims=True))
    return jnp.concatenate(blocks, axis=0)


def row_of(column):
    blocks = []
    for i in range(column.shape[0] // 128):
        part = jnp.broadcast_to(column[i * 128 : (i + 1) * 128], (128, 128))
        blocks.append(jnp.sum(jnp.where(eye(128), part, 0.0), axis=0, keepdims=True))
    return jnp.concatenate(blocks, axis=1)


def lanes_of(ref, first, count):
    return jnp.concatenate([ref[pl.ds(first + i, 1), :] for i in range(count)], axis=1)


def times_t(a, b, precision=None):
    return lax.dot_general(
        a, b, (((1,), (1,)), ((), ())), precision=precision, preferred_element_type=f32
    )


def t_times(a, b, precision=None):
    return lax.dot_general(
        a, b, (((0,), (0,)), ((), ())), precision=precision, preferred_element_type=f32
    )


def split3(y):
    high = y.astype(bf16).astype(f32)
    rest = y - high
    middle = rest.astype(bf16).astype(f32)
    return high, middle, rest - middle


def eight_rows(s_ref, c):
    sub = iota((8, 128), 0)
    rows = s_ref[c : c + 8, :]
    cols = [jnp.broadcast_to(rows[:, c + j : c + j + 1], (8, 128)) for j in range(8)]
    left, right = rows[:, :128], rows[:, 128:]
    for j in range(8):
        r = lax.rsqrt(jnp.broadcast_to(cols[j][j : j + 1, :], (8, 128)))
        f = jnp.where(sub > j, cols[j] * r, 0.0)
        own = jnp.where(sub == j, r, 1.0)
        for m in range(j + 1, 8):
            cols[m] = cols[m] - f * (jnp.broadcast_to(cols[m][j : j + 1, :], (8, 128)) * r)
        left_j = jnp.broadcast_to(left[j : j + 1, :], (8, 128)) * r
        right_j = jnp.broadcast_to(right[j : j + 1, :], (8, 128)) * r
        left = left * own - f * left_j
        right = right * own - f * right_j
    y = jnp.concatenate([left, right], axis=1)
    s_ref[c : c + 8, :] = y
    if c + 8 < 128:
        h, m, l = split3(y)
        lhs = jnp.concatenate([h, h, m, h, l, m], axis=0)[:, :128].astype(bf16)
        rhs = jnp.concatenate([h, m, h, l, h, m], axis=0).astype(bf16)
        s_ref[c + 8 :, :] = s_ref[c + 8 :, :] - t_times(lhs, rhs)[c + 8 :, :]


def factor_and_inverse(aug, s_ref, between):
    def block(k, carry):
        o = pl.multiple_of(k * 128, 128)
        s_ref[:, :128] = aug[pl.ds(o, 128), pl.ds(o, 128)]
        s_ref[:, 128:] = eye(128).astype(f32)
        for b in range(16):
            eight_rows(s_ref, 8 * b)
            between(k, b)
        aug[pl.ds(o, 128), :] = jnp.dot(
            s_ref[:, 128:], aug[pl.ds(o, 128), :], precision=HI, preferred_element_type=f32
        )
        for i in range(1, 4):

            @pl.when(i > k)
            def _():
                lhs = aug[pl.ds(o, 128), i * 128 : (i + 1) * 128]
                update = t_times(lhs, aug[pl.ds(o, 128), :], HI)
                aug[i * 128 : (i + 1) * 128, :] = aug[i * 128 : (i + 1) * 128, :] - update

        return carry

    lax.fori_loop(0, 4, block, 0)


def pick_pivots(scaled, pivot_column, first):
    waves = (first + iota((PANEL, COLS), 1)).astype(f32)
    taken = jnp.sum(jnp.where(pivot_column == waves, 1.0, 0.0), axis=0, keepdims=True)
    in_run = iota((MINE, COLS), 1) // RUN == iota((MINE, COLS), 0)
    one_hot = jnp.where(in_run, jnp.broadcast_to(taken, (MINE, COLS)), 0.0).astype(bf16)
    return jnp.dot(one_hot, scaled, preferred_element_type=f32).astype(bf16)


class Gather:
    def __init__(self, slot, sems, place, also=None):
        self.slot, self.sems, self.place, self.also = slot, sems, place, also
        y, c, x, z = place
        self.right_x, self.left_x = (y, c, lax.rem(x + 1, NX), z), (y, c, lax.rem(x + NX - 1, NX), z)
        self.right_z, self.left_z = (y, c, x, lax.rem(z + 1, NZ)), (y, c, x, lax.rem(z + NZ - 1, NZ))

    def z_at(self, j):
        z = self.place[3]
        return lax.rem(z + (NZ - j if j <= 4 else j - 4), NZ)

    def x_at(self, i):
        return lax.rem(self.place[2] + (0, NX - 1, 1, 2)[i], NX)

    def copy(self, ref, k, device):
        send, recv = self.sems
        return pltpu.make_async_remote_copy(ref, ref, send.at[k], recv.at[k], device, MESH_ID)

    def events(self, core):
        x, z = self.place[2], self.place[3]
        slot = self.slot
        out = []
        if core == 0:
            own = [(slot(x, z), 1, self.right_z), (slot(x, z), 5, self.left_z)]
            own += [(slot(x, z), 8, self.right_x), (slot(x, z), 16, self.left_x)]
            out.append((0.0, [], own, None))
            for j in range(1, 8):
                here = slot(x, self.z_at(j))
                sends = []
                if j in (1, 2, 3, 5, 6):
                    sends.append((here, j + 1, self.right_z if j < 4 else self.left_z))
                sends += [(here, 8 + j, self.right_x), (here, 16 + j, self.left_x)]
                steps = j if j <= 4 else j - 4
                out.append((1.0 * steps, [(here, j)], sends, (x, self.z_at(j))))
            for p, j in enumerate((0, 1, 5, 2, 6, 3, 7, 4)):
                zz = self.z_at(j)
                a, b, o = (self.x_at(i) for i in (1, 2, 3))
                out.append((1.3 + p * 0.9, [(slot(a, zz), 8 + j)], [(slot(a, zz, 0), 24 + j, self.right_x)], (a, zz)))
                out.append((1.3 + p * 0.9, [(slot(b, zz), 16 + j)], [(slot(b, zz, 1), 32 + j, self.left_x)], (b, zz)))
                halves = [(slot(o, zz, 0), 24 + j), (slot(o, zz, 1), 32 + j)]
                out.append((2.6 + p * 0.9, halves, [], (o, zz)))
        else:

            def along_z(i, step, side, ref):
                k = (4 if side == 0 else 20) + 4 * (step - 1) + i
                return (ref, k, self.right_z if side == 0 else self.left_z)

            own = [(slot(x, z), 0, self.right_x), (slot(x, z), 1, self.left_x)]
            own += [along_z(0, 1, side, slot(x, z)) for side in range(2)]
            out.append((0.0, [], own, None))
            for i in (1, 2, 3):
                xx = self.x_at(i)
                here = slot(xx, z)
                sends = [along_z(i, 1, side, here) for side in range(2)]
                waits = [(here, i - 1)]
                if i < 3:
                    sends.insert(0, (slot(xx, z, i - 1), i + 1, self.right_x if i == 1 else self.left_x))
                else:
                    waits = [(slot(xx, z, 0), 2), (slot(xx, z, 1), 3)]
                out.append((1.0 if i < 3 else 2.0, waits, sends, (xx, z)))
            for step in range(1, 5):
                for i in range(4):
                    for side in range(2 if step < 4 else 1):
                        zz = self.z_at(step + 4 * side)
                        here = slot(self.x_at(i), zz)
                        sends = [along_z(i, step + 1, side, here)] if step + side < 4 else []
                        k = (4 if side == 0 else 20) + 4 * (step - 1) + i
                        when = max(1.0 * step + (0, 1, 1, 2)[i], 1.05 + 2.0 * (step - 1) + 0.5 * i)
                        out.append((when, [(here, k)], sends, (self.x_at(i), zz)))
        return [e[1:] for e in sorted(out, key=lambda e: e[0])]

    def run(self, first, last=None):
        for core in range(2):

            @pl.when(self.place[1] == core)
            def _():
                for waits, sends, arrived in self.events(core)[first : first + 1 if last is None else last]:
                    for ref, k in waits:
                        self.copy(ref, k, self.right_x).wait_recv()
                    for ref, k, device in sends:
                        self.copy(ref, k, device).start()
                    if self.also is not None and arrived is not None:
                        self.also(*arrived).start()

    def drain(self):
        for core in range(2):

            @pl.when(self.place[1] == core)
            def _():
                for waits, sends, arrived in self.events(core):
                    for ref, k, device in sends:
                        self.copy(ref, k, device).wait_send()
                    if self.also is not None and arrived is not None:
                        self.also(*arrived).wait_send()


EVENTS = 32


def main_kernel(
    density_in,
    weight_in,
    coulomb_in,
    pivots_in,
    dielectric_ref,
    panel_ref,
    q_ref,
    r_ref,
    c_ref,
    qp_ref,
    aug,
    s_ref,
    columns_ref,
    density_ref,
    weight_ref,
    coulomb_ref,
    pivots_ref,
    scaled_ref,
    picked_ref,
    local_sem,
    qy_send,
    qy_recv,
    qg_send,
    qg_recv,
    rg_send,
    rg_recv,
    cy_send,
    cy_recv,
    one_send,
    one_recv,
    qx_send,
    qx_recv,
    cx_send,
    cx_recv,
):
    y, c, x, z = (lax.axis_index(a) for a in ("y", "c", "x", "z"))
    place = (y, c, x, z)
    partner = (y, 1 - c, x, z)

    def shift(plane, core):
        return lax.rem(plane + 12 - 4 * lax.rem(plane, 2) - 2 * core, NY)

    to_y, to_c = 2 * x + z // 4, lax.rem(z // 2, 2)
    to_half = lax.rem(z, 2)
    target = (to_y, to_c, 2 * to_half + c, lax.rem(y + NZ - shift(to_y, to_c), NZ))
    mine = shift(y, c)

    def owner_of(zz):
        return lax.rem(zz + mine, NY)

    origin = (owner_of(z), lax.rem(x, 2), y // 2, 4 * lax.rem(y, 2) + 2 * c + x // 2)

    def r_block(pair_core, half, owner):
        return r_ref.at[
            pair_core,
            pl.ds(pl.multiple_of(half * COLS, COLS), COLS),
            pl.ds(pl.multiple_of(owner * OWN, OWN), OWN),
        ]

    def r_slot(xx, zz, part=None):
        first, count = (xx // 2) * COLS, COLS
        if part is not None:
            first, count = first + part * (COLS // 2), COLS // 2
        return r_ref.at[
            lax.rem(xx, 2),
            pl.ds(pl.multiple_of(first, 256), count),
            pl.ds(pl.multiple_of(owner_of(zz) * OWN, OWN), OWN),
        ]

    def q_slot(xx, zz, part=None, core=None):
        rows = pl.ds(pl.multiple_of(zz * MINE, MINE), MINE)
        cols = slice(None) if part is None else pl.ds(part * (HALF // 2), HALF // 2)
        return q_ref.at[c if core is None else core, xx, rows, cols]

    def q_pass(xx, zz, back=False):
        ref, k = q_slot(xx, zz, core=1 - c if back else c), xx * NZ + zz
        return pltpu.make_async_remote_copy(ref, ref, qx_send.at[k], qx_recv.at[k], partner, MESH_ID)

    q_gather = Gather(q_slot, (qg_send, qg_recv), place, q_pass)
    r_gather = Gather(r_slot, (rg_send, rg_recv), place)

    barrier = pltpu.get_barrier_semaphore()
    greeted = [(lax.rem(y + d, NY), c, x, z) for d in range(1, NY)]
    greeted += [(y, c, x, lax.rem(z + d, NZ)) for d in (1, NZ - 1)]
    greeted += [(y, c, lax.rem(x + d, NX), z) for d in (1, NX - 1)]
    greeted += [partner, target, origin]
    for device in greeted:
        pl.semaphore_signal(barrier, 1, device_id=device, device_id_type=MESH_ID)

    inputs = [
        pltpu.make_async_copy(density_in, density_ref, local_sem.at[0]),
        pltpu.make_async_copy(weight_in, weight_ref, local_sem.at[1]),
        pltpu.make_async_copy(pivots_in, pivots_ref, local_sem.at[2]),
        pltpu.make_async_copy(coulomb_in, coulomb_ref, local_sem.at[3]),
    ]
    for copy in inputs:
        copy.start()
    for copy in inputs:
        copy.wait()
    pivot_row = jnp.concatenate([pivots_ref[i : i + 1, :] for i in range(4)], axis=1)
    first_col = (x * NZ + z) * COLS
    scaled = (density_ref[...].astype(f32) * jnp.sqrt(weight_ref[...])).astype(bf16)
    picked_own = pick_pivots(scaled, column_of(pivot_row.astype(f32)), first_col)
    own_rows = pl.ds(pl.multiple_of(z * MINE, MINE), MINE)
    own_pairs = pl.ds(pl.multiple_of(y * OWN, OWN), OWN)
    scaled_ref[...] = scaled
    picked_ref[...] = picked_own
    c_ref[c, :, own_pairs] = scaled
    q_ref[c, x, own_rows, own_pairs] = picked_own
    own_q = q_ref.at[c, x, own_rows, own_pairs]
    pl.semaphore_wait(barrier, len(greeted))

    def picked_copy(d):
        peer = (lax.rem(y + d, NY), c, x, z)
        return pltpu.make_async_remote_copy(
            picked_ref, own_q, qy_send.at[d], qy_recv.at[d], peer, MESH_ID
        )

    def picked_arrival(d):
        other = lax.rem(y + NY - d, NY)
        there = q_ref.at[c, x, own_rows, pl.ds(pl.multiple_of(other * OWN, OWN), OWN)]
        return pltpu.make_async_remote_copy(
            there, there, qy_send.at[d], qy_recv.at[d], partner, MESH_ID
        )

    for d in (4, 3, 5, 2, 6, 1, 7):
        picked_copy(d).start()

    spread = pltpu.make_async_remote_copy(
        scaled_ref, r_block(c, to_half, y), one_send.at[0], one_recv.at[0], target, MESH_ID
    )
    arrived = r_slot(x, z)
    spread_in = pltpu.make_async_remote_copy(
        arrived, arrived, one_send.at[0], one_recv.at[0], origin, MESH_ID
    )

    def c_of(owner):
        return c_ref.at[c, :, pl.ds(pl.multiple_of(owner * OWN, OWN), OWN)]

    def ring_y(step):
        up, down = (lax.rem(y + 1, NY), c, x, z), (lax.rem(y + NY - 1, NY), c, x, z)
        k = 2 * (step - 1)
        out = [(c_of(lax.rem(y + NY - step + 1, NY)), c_of(lax.rem(y + NY - step, NY)), k, up)]
        if step < 4:
            out.append((c_of(lax.rem(y + step - 1, NY)), c_of(lax.rem(y + step, NY)), k + 1, down))
        return out

    def c_copies(step, received):
        for sent, came, k, device in ring_y(step):
            ref = came if received else sent
            yield pltpu.make_async_remote_copy(ref, ref, cy_send.at[k], cy_recv.at[k], device, MESH_ID)

    def c_pass(owner, back=False):
        ref = c_ref.at[1 - c if back else c, :, pl.ds(pl.multiple_of(owner * OWN, OWN), OWN)]
        return pltpu.make_async_remote_copy(ref, ref, cx_send.at[owner], cx_recv.at[owner], partner, MESH_ID)

    def c_advance(event):
        if event > 1:
            for copy in c_copies(event - 1, True):
                copy.wait_recv()
            for away in (NY - event + 1, event - 1)[: 2 if event < 5 else 1]:
                c_pass(lax.rem(y + away, NY)).start()
        if event < 5:
            for copy in c_copies(event, False):
                copy.start()

    def repeat(count, do):
        def step(i, carry):
            do(i)
            return carry

        lax.fori_loop(0, count, step, 0)

    for d in range(1, NY):
        picked_arrival(d).wait_recv()
    q_gather.run(0)
    q_pass(x, z).start()
    spread.start()
    c_pass(y).start()
    c_advance(1)

    run_column = column_of((pivot_row // RUN).astype(f32))
    high_column = column_of((pivot_row // 128).astype(f32))
    low_column = column_of((pivot_row % 128).astype(f32))
    in_row = (high_column == iota((PANEL, 128), 1).astype(f32)).astype(f32)
    picked = jnp.dot(in_row, coulomb_ref[...], precision=HI, preferred_element_type=f32)
    at_lane = low_column == iota((PANEL, 128), 1).astype(f32)
    pivot_scale = jnp.sqrt(jnp.sum(jnp.where(at_lane, picked, 0.0), axis=1, keepdims=True))
    pivot_scale_row = row_of(pivot_scale)
    order = (run_column == iota((PANEL, PANEL), 1).astype(f32)).astype(bf16)

    q_gather.run(1, 20)
    c_advance(2)
    spread_in.wait_recv()
    r_gather.run(0)
    q_gather.run(20, EVENTS)
    repeat(NX * NZ, lambda i: q_pass(i // NZ, lax.rem(i, NZ), True).wait_recv())

    gram = None
    for h in range(2):
        qp_ref[h] = jnp.dot(
            order, q_ref[h].reshape(PANEL, HALF), preferred_element_type=f32
        ).astype(bf16)
        part = times_t(qp_ref[h], qp_ref[h])
        gram = part if gram is None else gram + part
    unit = eye(PANEL).astype(f32)
    aug[:, :PANEL] = pivot_scale * pivot_scale_row * gram + unit
    aug[:, PANEL:] = unit

    plan = {}
    for event in range(1, EVENTS):
        plan.setdefault((event - 1) * 25 // (EVENTS - 1), []).append(functools.partial(r_gather.run, event))
    for event, at in ((3, 3), (4, 8), (5, 13)):
        plan[at].append(functools.partial(c_advance, event))

    def between(k, b):
        if b % 2:
            return
        for block in range(4):
            todo = plan.get(8 * block + b // 2, ())
            if todo:

                @pl.when(k == block)
                def _():
                    for event in todo:
                        event()

    factor_and_inverse(aug, s_ref, between)

    lt = aug[:, :PANEL]
    row_i, col_i = iota((PANEL, PANEL), 0), iota((PANEL, PANEL), 1)
    diag = jnp.sum(jnp.where(row_i == col_i, lt, 0.0), axis=1, keepdims=True)
    upper = jnp.where(col_i >= row_i, lt * diag, 0.0)
    aug[:, PANEL:] = aug[:, PANEL:] / diag

    repeat(NY, lambda i: c_pass(i, True).wait_recv())

    first_row = (y * NC + c) * ROWS
    row_scale = jnp.sqrt(column_of(lanes_of(coulomb_ref, (y * NC + c) * 8, 8)))
    col_scale = jnp.sqrt(lanes_of(coulomb_ref, (x * NZ + z) * 4, 4))
    tile = 256
    for t in range(ROWS // tile):
        rows = slice(t * tile, (t + 1) * tile)
        scale = row_scale[rows]
        numbers = first_row + t * tile + iota((tile, COLS), 0)
        gram = times_t(r_ref[0, rows, :], c_ref[0]) + times_t(r_ref[1, rows, :], c_ref[1])
        same = numbers == first_col + iota((tile, COLS), 1)
        dielectric_ref[rows, :] = scale * col_scale * gram + jnp.where(same, 1.0, 0.0)
        gram = times_t(r_ref[0, rows, :], qp_ref[0]) + times_t(r_ref[1, rows, :], qp_ref[1])
        same = numbers == pivot_row
        columns_ref[...] = scale * pivot_scale_row * gram + jnp.where(same, 1.0, 0.0)
        panel_ref[rows, :256] = times_t(columns_ref[:, :256], aug[:256, PANEL : PANEL + 256], HI)
        panel_ref[rows, 256:] = times_t(columns_ref[...], aug[256:, PANEL:], HI)

    runs = ROWS // RUN
    run_row = pivot_row // RUN
    mine_here = run_row == (y * NC + c) * runs + iota((runs, PANEL), 0)
    pick = mine_here.astype(f32)
    top = jnp.dot(pick, upper, precision=HI, preferred_element_type=f32)
    position = jnp.sum(pick * iota((runs, PANEL), 1).astype(f32), axis=1, keepdims=True)
    within = jnp.sum(pick * jnp.broadcast_to((pivot_row % RUN).astype(f32), (runs, PANEL)), axis=1, keepdims=True)
    lane = iota((RUN, PANEL), 1).astype(f32)
    line = iota((RUN, PANEL), 0).astype(f32)
    for q in range(runs):
        rows = slice(q * RUN, (q + 1) * RUN)
        over = (line == within[q : q + 1]) & (lane >= position[q : q + 1])
        panel_ref[rows, :] = jnp.where(over, jnp.broadcast_to(top[q : q + 1, :], (RUN, PANEL)), panel_ref[rows, :])

    for d in range(1, NY):
        picked_copy(d).wait_send()
    spread.wait_send()
    for step in range(1, 5):
        for copy in c_copies(step, False):
            copy.wait_send()
    q_pass(x, z).wait_send()
    repeat(NY, lambda i: c_pass(i).wait_send())
    q_gather.drain()
    r_gather.drain()


def body(pair_density, pair_weight, coulomb, pivot_rows):
    vmem = pl.BlockSpec(memory_space=pltpu.VMEM)
    dma = pltpu.SemaphoreType.DMA
    return pl.pallas_call(
        main_kernel,
        out_shape=(
            jax.ShapeDtypeStruct((ROWS, COLS), f32),
            jax.ShapeDtypeStruct((ROWS, PANEL), f32),
        ),
        in_specs=[pl.BlockSpec(memory_space=pl.ANY)] * 4,
        out_specs=(vmem, vmem),
        scratch_shapes=[
            pltpu.VMEM((2, NX, NZ * MINE, HALF), bf16),
            pltpu.VMEM((2, ROWS, HALF), bf16),
            pltpu.VMEM((2, COLS, HALF), bf16),
            pltpu.VMEM((2, PANEL, HALF), bf16),
            pltpu.VMEM((PANEL, 2 * PANEL), f32),
            pltpu.VMEM((128, 256), f32),
            pltpu.VMEM((256, PANEL), f32),
            pltpu.VMEM((COLS, OWN), bf16),
            pltpu.VMEM((1, OWN), f32),
            pltpu.VMEM((128, 128), f32),
            pltpu.VMEM((4, 128), jnp.int32),
            pltpu.VMEM((COLS, OWN), bf16),
            pltpu.VMEM((MINE, OWN), bf16),
            dma((4,)),
            dma((NY,)),
            dma((NY,)),
            dma((40,)),
            dma((40,)),
            dma((40,)),
            dma((40,)),
            dma((7,)),
            dma((7,)),
            dma((1,)),
            dma((1,)),
            dma((NX * NZ,)),
            dma((NX * NZ,)),
            dma((NY,)),
            dma((NY,)),
        ],
        compiler_params=pltpu.CompilerParams(
            collective_id=0, has_side_effects=True, vmem_limit_bytes=40 * 2**20
        ),
        name="gather_factor_panel",
    )(pair_density, pair_weight.reshape(1, OWN), coulomb.reshape(128, 128), pivot_rows.reshape(4, 128))


def solution(mesh):
    finer = Mesh(mesh.devices.reshape(NY, NC, NX, NZ), ("y", "c", "x", "z"))
    return jax.shard_map(
        body,
        mesh=finer,
        in_specs=(P(("x", "z"), ("y", "c")), P(("y", "c")), P(), P()),
        out_specs=(P(("y", "c"), ("x", "z")), P(("y", "c"), None)),
        check_vma=False,
    )
```

```python
import functools

import jax
import jax.numpy as jnp
from jax import lax
from jax.experimental import pallas as pl
from jax.experimental.pallas import tpu as pltpu
from jax.sharding import Mesh
from jax.sharding import PartitionSpec as P

NG = 16384
PANEL = 512
RUN = NG // PANEL
NY, NC, NX, NZ = 8, 2, 4, 8
COLS = NG // (NX * NZ)
ROWS = NG // (NY * NC)
OWN = 128
HALF = NY * OWN
MINE = COLS // RUN
HI = lax.Precision.HIGHEST
f32, bf16 = jnp.float32, jnp.bfloat16
MESH_ID = pl.DeviceIdType.MESH


def iota(shape, dim):
    return lax.broadcasted_iota(jnp.int32, shape, dim)


def eye(n):
    return iota((n, n), 0) == iota((n, n), 1)


def column_of(row):
    blocks = []
    for i in range(row.shape[1] // 128):
        part = jnp.broadcast_to(row[:, i * 128 : (i + 1) * 128], (128, 128))
        blocks.append(jnp.sum(jnp.where(eye(128), part, 0.0), axis=1, keepdims=True))
    return jnp.concatenate(blocks, axis=0)


def row_of(column):
    blocks = []
    for i in range(column.shape[0] // 128):
        part = jnp.broadcast_to(column[i * 128 : (i + 1) * 128], (128, 128))
        blocks.append(jnp.sum(jnp.where(eye(128), part, 0.0), axis=0, keepdims=True))
    return jnp.concatenate(blocks, axis=1)


def lanes_of(ref, first, count):
    return jnp.concatenate([ref[pl.ds(first + i, 1), :] for i in range(count)], axis=1)


def times_t(a, b, precision=None):
    return lax.dot_general(
        a, b, (((1,), (1,)), ((), ())), precision=precision, preferred_element_type=f32
    )


def t_times(a, b, precision=None):
    return lax.dot_general(
        a, b, (((0,), (0,)), ((), ())), precision=precision, preferred_element_type=f32
    )


def split3(y):
    high = y.astype(bf16).astype(f32)
    rest = y - high
    middle = rest.astype(bf16).astype(f32)
    return high, middle, rest - middle


def eight_rows(s_ref, c):
    sub = iota((8, 128), 0)

    def taken(first):
        rows = s_ref[first : first + 8, :]
        cols = [jnp.broadcast_to(rows[:, c + j : c + j + 1], (8, 128)) for j in range(8)]
        return [cols, rows[:, :128], rows[:, 128:]]

    ahead = [first for first in (c + 8, c + 16) if first < 128]
    cols, left, right = taken(c)
    later = [taken(first) for first in ahead]
    for j in range(8):
        r = lax.rsqrt(jnp.broadcast_to(cols[j][j : j + 1, :], (8, 128)))
        f = jnp.where(sub > j, cols[j] * r, 0.0)
        own = jnp.where(sub == j, r, 1.0)
        factors = [part[0][j] * r for part in later]
        for m in range(j + 1, 8):
            pivot = jnp.broadcast_to(cols[m][j : j + 1, :], (8, 128)) * r
            cols[m] = cols[m] - f * pivot
            for part, g in zip(later, factors):
                part[0][m] = part[0][m] - g * pivot
        left_j = jnp.broadcast_to(left[j : j + 1, :], (8, 128)) * r
        right_j = jnp.broadcast_to(right[j : j + 1, :], (8, 128)) * r
        left = left * own - f * left_j
        right = right * own - f * right_j
        for part, g in zip(later, factors):
            part[1] = part[1] - g * left_j
            part[2] = part[2] - g * right_j
    y = jnp.concatenate([left, right], axis=1)
    s_ref[c : c + 8, :] = y
    for first, part in zip(ahead, later):
        s_ref[first : first + 8, :] = jnp.concatenate(part[1:], axis=1)
    rest = c + 24
    if rest < 128:
        h, m, l = split3(y)
        lhs = jnp.concatenate([h, h, m, h, l, m], axis=0)[:, :128].astype(bf16)
        rhs = jnp.concatenate([h, m, h, l, h, m], axis=0).astype(bf16)
        s_ref[rest:, :] = s_ref[rest:, :] - t_times(lhs, rhs)[rest:, :]


def factor_and_inverse(aug, s_ref, between):
    def block(k, carry):
        o = pl.multiple_of(k * 128, 128)
        span = pl.ds(o, PANEL + 128)
        s_ref[:, :128] = aug[pl.ds(o, 128), pl.ds(o, 128)]
        s_ref[:, 128:] = eye(128).astype(f32)
        for b in range(16):
            if b % 4 == 0:
                between(k, b // 4)
            eight_rows(s_ref, 8 * b)
        aug[pl.ds(o, 128), span] = jnp.dot(
            s_ref[:, 128:], aug[pl.ds(o, 128), span], precision=HI, preferred_element_type=f32
        )
        for i in range(1, 4):

            @pl.when(i > k)
            def _():
                lhs = aug[pl.ds(o, 128), i * 128 : (i + 1) * 128]
                update = t_times(lhs, aug[pl.ds(o, 128), span], HI)
                aug[i * 128 : (i + 1) * 128, span] = aug[i * 128 : (i + 1) * 128, span] - update

        return carry

    lax.fori_loop(0, 4, block, 0)


def pick_pivots(scaled, pivot_column, first):
    waves = (first + iota((PANEL, COLS), 1)).astype(f32)
    taken = jnp.sum(jnp.where(pivot_column == waves, 1.0, 0.0), axis=0, keepdims=True)
    in_run = iota((MINE, COLS), 1) // RUN == iota((MINE, COLS), 0)
    one_hot = jnp.where(in_run, jnp.broadcast_to(taken, (MINE, COLS)), 0.0).astype(bf16)
    return jnp.dot(one_hot, scaled, preferred_element_type=f32).astype(bf16)


class Gather:
    def __init__(self, sems, place):
        self.sems, self.place = sems, place
        y, c, x, z = place
        self.right_x, self.left_x = self.to_x(1), self.to_x(NX - 1)
        self.right_z, self.left_z = self.to_z(1), self.to_z(NZ - 1)

    def to_x(self, d):
        y, c, x, z = self.place
        return (y, c, lax.rem(x + d, NX), z)

    def to_z(self, d):
        y, c, x, z = self.place
        return (y, c, x, lax.rem(z + d, NZ))

    def z_at(self, j):
        z = self.place[3]
        return lax.rem(z + (NZ - j if j <= 4 else j - 4), NZ)

    def x_at(self, i):
        return lax.rem(self.place[2] + (0, NX - 1, 1, 2)[i], NX)

    def copy(self, ref, k, device):
        send, recv = self.sems
        return pltpu.make_async_remote_copy(ref, ref, send.at[k], recv.at[k], device, MESH_ID)

    def run(self, first, last=None):
        for core in range(2):

            @pl.when(self.place[1] == core)
            def _():
                for waits, sends, passes in self.events(core)[first : first + 1 if last is None else last]:
                    for ref, k in waits:
                        self.copy(ref, k, self.right_x).wait_recv()
                    for ref, k, device in sends:
                        self.copy(ref, k, device).start()
                    for line in passes:
                        self.line(*line).start()

    def drain(self):
        for core in range(2):

            @pl.when(self.place[1] == core)
            def _():
                for waits, sends, passes in self.events(core):
                    for ref, k, device in sends:
                        self.copy(ref, k, device).wait_send()
                    for line in passes:
                        self.line(*line).wait_send()


class PivotGather(Gather):
    def __init__(self, q_ref, sems, pass_sems, place):
        super().__init__(sems, place)
        self.q_ref, self.pass_sems = q_ref, pass_sems

    def at(self, xs, z=None, core=None, rows=None):
        if z is not None:
            rows = pl.ds(pl.multiple_of(z * MINE, MINE), MINE)
        return self.q_ref.at[self.place[1] if core is None else core, xs, slice(None) if rows is None else rows, :]

    def passed(self, ref, k):
        send, recv = self.pass_sems
        y, c, x, z = self.place
        return pltpu.make_async_remote_copy(ref, ref, send.at[k], recv.at[k], (y, 1 - c, x, z), MESH_ID)

    def line(self, core, i, back=False):
        owner = 1 - self.place[1] if back else self.place[1]
        return self.passed(self.at(i, core=owner) if core == 0 else self.at(slice(None), i, core=owner), i)

    def wait_passed(self):
        for core in range(2):

            @pl.when(self.place[1] == core)
            def _():
                def step(i, carry):
                    self.line(1 - core, i, True).wait_recv()
                    return carry

                lax.fori_loop(0, NZ if core == 0 else NX, step, 0)

    def events(self, core):
        x, z = self.place[2:]
        everything = slice(None)
        if core == 0:
            start = [(self.at(x, z), d, self.to_z(d)) for d in (4, 3, 5, 2, 6, 1, 7)]
            arrive = [(self.at(x, lax.rem(z + NZ - d, NZ)), d) for d in range(1, NZ)]
            mine, a, b, o = (self.x_at(i) for i in range(4))
            whole = [(self.at(mine), 8, self.right_x), (self.at(mine), 9, self.left_x)]
            low, high = pl.ds(0, 64), pl.ds(64, 64)
            first = ([(self.at(a), 8)], [(self.at(a, rows=low), 10, self.right_x)], [(0, a)])
            second = ([(self.at(b), 9)], [(self.at(b, rows=high), 11, self.left_x)], [(0, b)])
            both = [(self.at(o, rows=low), 10), (self.at(o, rows=high), 11)]
            none = ([], [], [])
            return [([], start, []), none, none, (arrive, whole, [(0, mine)]), none, first, second, none, (both, [], [(0, o)])]

        def part(zz, m):
            return self.at(pl.ds(2 * m, 2), zz)

        def key(step, m, side):
            return 4 + 4 * (step - 1) + 2 * m + side

        def onward(step, zz, m):
            out = []
            if step < 4 or m == 0:
                out.append((part(zz[0], m), key(step, m, 0), self.right_z))
            if step < 4 or m == 1:
                out.append((part(zz[1], m), key(step, m, 1), self.left_z))
            return out

        start = [(self.at(x, z), d, self.to_x(d)) for d in (2, 1, 3)]
        arrive = [(self.at(lax.rem(x + NX - d, NX), z), d) for d in range(1, NX)]
        out = [([], start, []), (arrive, onward(1, (z, z), 0) + onward(1, (z, z), 1), [(1, z)])]
        for step in (1, 2, 3):
            zz = self.z_at(step), self.z_at(step + 4)
            for m in range(2):
                waits = [(part(zz[side], m), key(step, m, side)) for side in range(2)]
                out.append((waits, onward(step + 1, zz, m), [(1, zz[side]) for side in range(2)] if m else []))
        far = self.z_at(4)
        out.append(([(part(far, 0), key(4, 0, 0)), (part(far, 1), key(4, 1, 1))], [], [(1, far)]))
        return out


class RowGather(Gather):
    RIGHT = ((1, 0), (2, 0), (1, 1), (1, 2), (1, 3), (3, 0), (2, 1), (2, 2), (2, 3), (4, 0), (3, 1), (3, 2), (3, 3), (4, 1))
    LEFT = ((1, 0), (2, 0), (1, 1), (1, 2), (1, 3), (3, 0), (2, 1), (2, 2), (2, 3), (3, 1), (3, 2), (4, 2), (3, 3), (4, 3))

    def __init__(self, slot, sems, place):
        super().__init__(sems, place)
        self.slot = slot

    def events(self, core):
        x, z = self.place[2:]
        slot = self.slot
        out = []
        if core == 0:
            own = [(slot(x, z), 1, self.right_z), (slot(x, z), 5, self.left_z)]
            own += [(slot(x, z), 8, self.right_x), (slot(x, z), 16, self.left_x)]
            out.append(([], own, []))
            order = (0, 1, 5, 2, 6, 3, 7, 4)

            def along_z(j):
                here = slot(x, self.z_at(j))
                waits, sends = [(here, j)], []
                if j == 4:
                    waits = [(slot(x, self.z_at(4), 0), 4), (slot(x, self.z_at(4), 1), 32)]
                elif j == 3:
                    sends = [(slot(x, self.z_at(3), 0), 4, self.right_z)]
                elif j == 7:
                    sends = [(slot(x, self.z_at(7), 1), 32, self.left_z)]
                else:
                    sends = [(here, j + 1, self.right_z if j < 4 else self.left_z)]
                return waits, sends + [(here, 8 + j, self.right_x), (here, 16 + j, self.left_x)], []

            def along_x(p, side):
                j = order[p]
                here = slot(self.x_at(1 + side), self.z_at(j) if j else z)
                sends = [(here, 24 + j, self.left_x if side else self.right_x)] if p % 2 == side else []
                return [(here, (16 if side else 8) + j)], sends, []

            def opposite(p):
                j = order[p]
                return [(slot(self.x_at(3), self.z_at(j) if j else z), 24 + j)], [], []

            out += [along_z(1), along_z(5), along_x(0, 0), along_x(0, 1), along_z(2), along_z(6)]
            out += [along_x(1, 0), along_x(1, 1), opposite(0), along_z(3), along_z(7)]
            out += [along_x(2, 0), along_x(2, 1), opposite(1), along_z(4)]
            for p in range(3, 8):
                out += [along_x(p, 0), along_x(p, 1), opposite(p - 1)]
            out.append(opposite(7))
            return out

        def key(step, i, side):
            return 4 + 8 * (step - 1) + 2 * i + side

        def onward(step, i, side, here):
            if step > 4 or (step == 4 and i // 2 != side):
                return []
            return [(here, key(step, i, side), self.left_z if side else self.right_z)]

        def along(step, i, side):
            here = slot(self.x_at(i), self.z_at(step + 4 * side if step < 4 else 4))
            return [(here, key(step, i, side))], onward(step + 1, i, side, here), []

        own = [(slot(x, z), d, self.to_x(d)) for d in (2, 1, 3)]
        out.append(([], own + onward(1, 0, 0, slot(x, z)) + onward(1, 0, 1, slot(x, z)), []))
        right, left = list(self.RIGHT), list(self.LEFT)
        out += [along(*right.pop(0), 0), along(*left.pop(0), 1)]
        for i, d in ((1, 1), (2, 3), (3, 2)):
            here = slot(self.x_at(i), z)
            out.append(([(here, d)], onward(1, i, 0, here) + onward(1, i, 1, here), []))
        while right:
            out += [along(*right.pop(0), 0), along(*left.pop(0), 1)]
        return out


EVENTS = 32


def main_kernel(
    density_in,
    weight_in,
    coulomb_in,
    pivots_in,
    dielectric_ref,
    panel_ref,
    q_ref,
    r_ref,
    c_ref,
    qp_ref,
    aug,
    s_ref,
    columns_ref,
    density_ref,
    weight_ref,
    coulomb_ref,
    pivots_ref,
    scaled_ref,
    picked_ref,
    local_sem,
    qy_send,
    qy_recv,
    qg_send,
    qg_recv,
    rg_send,
    rg_recv,
    cy_send,
    cy_recv,
    one_send,
    one_recv,
    qx_send,
    qx_recv,
    cx_send,
    cx_recv,
):
    y, c, x, z = (lax.axis_index(a) for a in ("y", "c", "x", "z"))
    place = (y, c, x, z)
    partner = (y, 1 - c, x, z)

    def shift(plane, core):
        return lax.rem(plane + 12 - 4 * lax.rem(plane, 2) - 2 * core, NY)

    to_y, to_c = 2 * x + z // 4, lax.rem(z // 2, 2)
    to_half = lax.rem(z, 2)
    target = (to_y, to_c, 2 * to_half + c, lax.rem(y + NZ - shift(to_y, to_c), NZ))
    mine = shift(y, c)

    def owner_of(zz):
        return lax.rem(zz + mine, NY)

    origin = (owner_of(z), lax.rem(x, 2), y // 2, 4 * lax.rem(y, 2) + 2 * c + x // 2)

    def r_block(pair_core, half, owner):
        return r_ref.at[
            pair_core,
            pl.ds(pl.multiple_of(half * COLS, COLS), COLS),
            pl.ds(pl.multiple_of(owner * OWN, OWN), OWN),
        ]

    def r_slot(xx, zz, part=None):
        first, count = (xx // 2) * COLS, COLS
        if part is not None:
            first, count = first + part * (COLS // 2), COLS // 2
        return r_ref.at[
            lax.rem(xx, 2),
            pl.ds(pl.multiple_of(first, 256), count),
            pl.ds(pl.multiple_of(owner_of(zz) * OWN, OWN), OWN),
        ]

    q_gather = PivotGather(q_ref, (qg_send, qg_recv), (qx_send, qx_recv), place)
    r_gather = RowGather(r_slot, (rg_send, rg_recv), place)

    barrier = pltpu.get_barrier_semaphore()
    greeted = [(lax.rem(y + d, NY), c, x, z) for d in range(1, NY)]
    greeted += [(y, c, x, lax.rem(z + d, NZ)) for d in range(1, NZ)]
    greeted += [(y, c, lax.rem(x + d, NX), z) for d in range(1, NX)]
    greeted += [partner, target, origin]
    for device in greeted:
        pl.semaphore_signal(barrier, 1, device_id=device, device_id_type=MESH_ID)

    inputs = [
        pltpu.make_async_copy(density_in, density_ref, local_sem.at[0]),
        pltpu.make_async_copy(weight_in, weight_ref, local_sem.at[1]),
        pltpu.make_async_copy(pivots_in, pivots_ref, local_sem.at[2]),
        pltpu.make_async_copy(coulomb_in, coulomb_ref, local_sem.at[3]),
    ]
    for copy in inputs:
        copy.start()
    for copy in inputs:
        copy.wait()
    pivot_row = jnp.concatenate([pivots_ref[i : i + 1, :] for i in range(4)], axis=1)
    first_col = (x * NZ + z) * COLS
    scaled = (density_ref[...].astype(f32) * jnp.sqrt(weight_ref[...])).astype(bf16)
    picked_own = pick_pivots(scaled, column_of(pivot_row.astype(f32)), first_col)
    own_rows = pl.ds(pl.multiple_of(z * MINE, MINE), MINE)
    own_pairs = pl.ds(pl.multiple_of(y * OWN, OWN), OWN)
    scaled_ref[...] = scaled
    picked_ref[...] = picked_own
    c_ref[c, :, own_pairs] = scaled
    q_ref[c, x, own_rows, own_pairs] = picked_own
    own_q = q_ref.at[c, x, own_rows, own_pairs]
    pl.semaphore_wait(barrier, len(greeted))

    def picked_copy(d):
        peer = (lax.rem(y + d, NY), c, x, z)
        return pltpu.make_async_remote_copy(
            picked_ref, own_q, qy_send.at[d], qy_recv.at[d], peer, MESH_ID
        )

    def picked_arrival(d):
        other = lax.rem(y + NY - d, NY)
        there = q_ref.at[c, x, own_rows, pl.ds(pl.multiple_of(other * OWN, OWN), OWN)]
        return pltpu.make_async_remote_copy(
            there, there, qy_send.at[d], qy_recv.at[d], partner, MESH_ID
        )

    for d in (4, 3, 5, 2, 6, 1, 7):
        picked_copy(d).start()

    spread = pltpu.make_async_remote_copy(
        scaled_ref, r_block(c, to_half, y), one_send.at[0], one_recv.at[0], target, MESH_ID
    )
    arrived = r_slot(x, z)
    spread_in = pltpu.make_async_remote_copy(
        arrived, arrived, one_send.at[0], one_recv.at[0], origin, MESH_ID
    )

    def c_of(owner):
        return c_ref.at[c, :, pl.ds(pl.multiple_of(owner * OWN, OWN), OWN)]

    def ring_y(step):
        up, down = (lax.rem(y + 1, NY), c, x, z), (lax.rem(y + NY - 1, NY), c, x, z)
        k = 2 * (step - 1)
        out = [(c_of(lax.rem(y + NY - step + 1, NY)), c_of(lax.rem(y + NY - step, NY)), k, up)]
        if step < 4:
            out.append((c_of(lax.rem(y + step - 1, NY)), c_of(lax.rem(y + step, NY)), k + 1, down))
        return out

    def c_copies(step, received):
        for sent, came, k, device in ring_y(step):
            ref = came if received else sent
            yield pltpu.make_async_remote_copy(ref, ref, cy_send.at[k], cy_recv.at[k], device, MESH_ID)

    def c_pass(owner, back=False):
        ref = c_ref.at[1 - c if back else c, :, pl.ds(pl.multiple_of(owner * OWN, OWN), OWN)]
        return pltpu.make_async_remote_copy(ref, ref, cx_send.at[owner], cx_recv.at[owner], partner, MESH_ID)

    def c_advance(event):
        if event > 1:
            for copy in c_copies(event - 1, True):
                copy.wait_recv()
            for away in (NY - event + 1, event - 1)[: 2 if event < 5 else 1]:
                c_pass(lax.rem(y + away, NY)).start()
        if event < 5:
            for copy in c_copies(event, False):
                copy.start()

    def repeat(count, do):
        def step(i, carry):
            do(i)
            return carry

        lax.fori_loop(0, count, step, 0)

    spread.start()
    c_pass(y).start()
    c_advance(1)

    run_column = column_of((pivot_row // RUN).astype(f32))
    high_column = column_of((pivot_row // 128).astype(f32))
    low_column = column_of((pivot_row % 128).astype(f32))
    in_row = (high_column == iota((PANEL, 128), 1).astype(f32)).astype(f32)
    picked = jnp.dot(in_row, coulomb_ref[...], precision=HI, preferred_element_type=f32)
    at_lane = low_column == iota((PANEL, 128), 1).astype(f32)
    pivot_scale = jnp.sqrt(jnp.sum(jnp.where(at_lane, picked, 0.0), axis=1, keepdims=True))
    pivot_scale_row = row_of(pivot_scale)
    order = (run_column == iota((PANEL, PANEL), 1).astype(f32)).astype(bf16)

    for d in range(1, NY):
        picked_arrival(d).wait_recv()
    q_gather.run(0)
    c_advance(2)
    q_gather.run(1, 3)
    spread_in.wait_recv()
    r_gather.run(0)
    q_gather.run(3)
    c_advance(3)
    q_gather.run(4, 6)
    r_gather.run(1, 3)
    q_gather.run(6)
    c_advance(4)
    r_gather.run(3, 5)
    q_gather.run(7, 9)
    q_gather.wait_passed()

    gram = None
    for h in range(2):
        qp_ref[h] = jnp.dot(
            order, q_ref[h].reshape(PANEL, HALF), preferred_element_type=f32
        ).astype(bf16)
        part = times_t(qp_ref[h], qp_ref[h])
        gram = part if gram is None else gram + part
    unit = eye(PANEL).astype(f32)
    aug[:, :PANEL] = pivot_scale * pivot_scale_row * gram + unit
    aug[:, PANEL:] = unit
    r_gather.run(5, 11)
    c_advance(5)

    def between(k, part):
        for block in range(4):
            at = 4 * block + part
            first, last = (min(EVENTS, 11 + (21 * i) // 13) for i in (at, at + 1))
            if first < last:

                @pl.when(k == block)
                def _():
                    r_gather.run(first, last)

    factor_and_inverse(aug, s_ref, between)

    diag = jnp.concatenate(
        [
            jnp.sum(jnp.where(eye(128), aug[i : i + 128, i : i + 128], 0.0), axis=1, keepdims=True)
            for i in range(0, PANEL, 128)
        ],
        axis=0,
    )
    aug[:, PANEL:] = aug[:, PANEL:] / diag

    runs = ROWS // RUN
    run_row = pivot_row // RUN
    pick = (run_row == (y * NC + c) * runs + iota((runs, PANEL), 0)).astype(f32)
    top = None
    for part in split3(aug[:, :PANEL]):
        rows = jnp.dot(pick.astype(bf16), part.astype(bf16), preferred_element_type=f32)
        top = rows if top is None else top + rows
    top = top * jnp.sum(pick * row_of(diag), axis=1, keepdims=True)
    position = jnp.sum(pick * iota((runs, PANEL), 1).astype(f32), axis=1, keepdims=True)
    within = jnp.sum(pick * (pivot_row % RUN).astype(f32), axis=1, keepdims=True)

    repeat(NY, lambda i: c_pass(i, True).wait_recv())

    first_row = (y * NC + c) * ROWS
    row_scale = jnp.sqrt(column_of(lanes_of(coulomb_ref, (y * NC + c) * 8, 8)))
    col_scale = jnp.sqrt(lanes_of(coulomb_ref, (x * NZ + z) * 4, 4))
    tile = 256
    for t in range(ROWS // tile):
        rows = slice(t * tile, (t + 1) * tile)
        scale = row_scale[rows]
        numbers = first_row + t * tile + iota((tile, COLS), 0)
        gram = times_t(r_ref[0, rows, :], c_ref[0]) + times_t(r_ref[1, rows, :], c_ref[1])
        same = numbers == first_col + iota((tile, COLS), 1)
        dielectric_ref[rows, :] = scale * col_scale * gram + jnp.where(same, 1.0, 0.0)
        gram = times_t(r_ref[0, rows, :], qp_ref[0]) + times_t(r_ref[1, rows, :], qp_ref[1])
        same = numbers == pivot_row
        columns_ref[...] = scale * pivot_scale_row * gram + jnp.where(same, 1.0, 0.0)
        panel_ref[rows, :256] = times_t(columns_ref[:, :256], aug[:256, PANEL : PANEL + 256], HI)
        panel_ref[rows, 256:] = times_t(columns_ref[...], aug[256:, PANEL:], HI)

    lane = iota((RUN, PANEL), 1).astype(f32)
    line = iota((RUN, PANEL), 0).astype(f32)
    for q in range(runs):
        rows = slice(q * RUN, (q + 1) * RUN)
        over = (line == within[q : q + 1]) & (lane >= position[q : q + 1])
        panel_ref[rows, :] = jnp.where(over, jnp.broadcast_to(top[q : q + 1, :], (RUN, PANEL)), panel_ref[rows, :])

    for d in range(1, NY):
        picked_copy(d).wait_send()
    spread.wait_send()
    for step in range(1, 5):
        for copy in c_copies(step, False):
            copy.wait_send()
    repeat(NY, lambda i: c_pass(i).wait_send())
    q_gather.drain()
    r_gather.drain()


def body(pair_density, pair_weight, coulomb, pivot_rows):
    vmem = pl.BlockSpec(memory_space=pltpu.VMEM)
    dma = pltpu.SemaphoreType.DMA
    return pl.pallas_call(
        main_kernel,
        out_shape=(
            jax.ShapeDtypeStruct((ROWS, COLS), f32),
            jax.ShapeDtypeStruct((ROWS, PANEL), f32),
        ),
        in_specs=[pl.BlockSpec(memory_space=pl.ANY)] * 4,
        out_specs=(vmem, vmem),
        scratch_shapes=[
            pltpu.VMEM((2, NX, NZ * MINE, HALF), bf16),
            pltpu.VMEM((2, ROWS, HALF), bf16),
            pltpu.VMEM((2, COLS, HALF), bf16),
            pltpu.VMEM((2, PANEL, HALF), bf16),
            pltpu.VMEM((PANEL, 2 * PANEL), f32),
            pltpu.VMEM((128, 256), f32),
            pltpu.VMEM((256, PANEL), f32),
            pltpu.VMEM((COLS, OWN), bf16),
            pltpu.VMEM((1, OWN), f32),
            pltpu.VMEM((128, 128), f32),
            pltpu.VMEM((4, 128), jnp.int32),
            pltpu.VMEM((COLS, OWN), bf16),
            pltpu.VMEM((MINE, OWN), bf16),
            dma((4,)),
            dma((NY,)),
            dma((NY,)),
            dma((20,)),
            dma((20,)),
            dma((36,)),
            dma((36,)),
            dma((7,)),
            dma((7,)),
            dma((1,)),
            dma((1,)),
            dma((NZ,)),
            dma((NZ,)),
            dma((NY,)),
            dma((NY,)),
        ],
        compiler_params=pltpu.CompilerParams(
            collective_id=0, has_side_effects=True, vmem_limit_bytes=40 * 2**20
        ),
        name="gather_factor_panel",
    )(pair_density, pair_weight.reshape(1, OWN), coulomb.reshape(128, 128), pivot_rows.reshape(4, 128))


def solution(mesh):
    finer = Mesh(mesh.devices.reshape(NY, NC, NX, NZ), ("y", "c", "x", "z"))
    return jax.shard_map(
        body,
        mesh=finer,
        in_specs=(P(("x", "z"), ("y", "c")), P(("y", "c")), P(), P()),
        out_specs=(P(("y", "c"), ("x", "z")), P(("y", "c"), None)),
        check_vma=False,
    )
```

```python
import functools

import jax
import jax.numpy as jnp
from jax import lax
from jax.experimental import pallas as pl
from jax.experimental.pallas import tpu as pltpu
from jax.sharding import Mesh
from jax.sharding import PartitionSpec as P

NG = 16384
PANEL = 512
RUN = NG // PANEL
NY, NC, NX, NZ = 8, 2, 4, 8
COLS = NG // (NX * NZ)
ROWS = NG // (NY * NC)
OWN = 128
HALF = NY * OWN
MINE = COLS // RUN
HI = lax.Precision.HIGHEST
f32, bf16 = jnp.float32, jnp.bfloat16
MESH_ID = pl.DeviceIdType.MESH


def iota(shape, dim):
    return lax.broadcasted_iota(jnp.int32, shape, dim)


def eye(n):
    return iota((n, n), 0) == iota((n, n), 1)


def column_of(row):
    blocks = []
    for i in range(row.shape[1] // 128):
        part = jnp.broadcast_to(row[:, i * 128 : (i + 1) * 128], (128, 128))
        blocks.append(jnp.sum(jnp.where(eye(128), part, 0.0), axis=1, keepdims=True))
    return jnp.concatenate(blocks, axis=0)


def row_of(column):
    blocks = []
    for i in range(column.shape[0] // 128):
        part = jnp.broadcast_to(column[i * 128 : (i + 1) * 128], (128, 128))
        blocks.append(jnp.sum(jnp.where(eye(128), part, 0.0), axis=0, keepdims=True))
    return jnp.concatenate(blocks, axis=1)


def lanes_of(ref, first, count):
    return jnp.concatenate([ref[pl.ds(first + i, 1), :] for i in range(count)], axis=1)


def times_t(a, b, precision=None):
    return lax.dot_general(
        a, b, (((1,), (1,)), ((), ())), precision=precision, preferred_element_type=f32
    )


def t_times(a, b, precision=None):
    return lax.dot_general(
        a, b, (((0,), (0,)), ((), ())), precision=precision, preferred_element_type=f32
    )


def split3(y):
    high = y.astype(bf16).astype(f32)
    rest = y - high
    middle = rest.astype(bf16).astype(f32)
    return high, middle, rest - middle


def eight_rows(s_ref, c):
    sub = iota((8, 128), 0)

    def taken(first):
        rows = s_ref[first : first + 8, :]
        cols = [jnp.broadcast_to(rows[:, c + j : c + j + 1], (8, 128)) for j in range(8)]
        return [cols, rows[:, :128], rows[:, 128:]]

    ahead = [first for first in (c + 8, c + 16) if first < 128]
    cols, left, right = taken(c)
    later = [taken(first) for first in ahead]
    for j in range(8):
        r = lax.rsqrt(jnp.broadcast_to(cols[j][j : j + 1, :], (8, 128)))
        f = jnp.where(sub > j, cols[j] * r, 0.0)
        own = jnp.where(sub == j, r, 1.0)
        factors = [part[0][j] * r for part in later]
        for m in range(j + 1, 8):
            pivot = jnp.broadcast_to(cols[m][j : j + 1, :], (8, 128)) * r
            cols[m] = cols[m] - f * pivot
            for part, g in zip(later, factors):
                part[0][m] = part[0][m] - g * pivot
        left_j = jnp.broadcast_to(left[j : j + 1, :], (8, 128)) * r
        right_j = jnp.broadcast_to(right[j : j + 1, :], (8, 128)) * r
        left = left * own - f * left_j
        right = right * own - f * right_j
        for part, g in zip(later, factors):
            part[1] = part[1] - g * left_j
            part[2] = part[2] - g * right_j
    y = jnp.concatenate([left, right], axis=1)
    s_ref[c : c + 8, :] = y
    for first, part in zip(ahead, later):
        s_ref[first : first + 8, :] = jnp.concatenate(part[1:], axis=1)
    rest = c + 24
    if rest < 128:
        h, m, l = split3(y)
        lhs = jnp.concatenate([h, h, m, h, l, m], axis=0)[:, :128].astype(bf16)
        rhs = jnp.concatenate([h, m, h, l, h, m], axis=0).astype(bf16)
        s_ref[rest:, :] = s_ref[rest:, :] - t_times(lhs, rhs)[rest:, :]


def factor_and_inverse(aug, s_ref, between):
    def block(k, carry):
        o = pl.multiple_of(k * 128, 128)
        span = pl.ds(o, PANEL + 128)
        s_ref[:, :128] = aug[pl.ds(o, 128), pl.ds(o, 128)]
        s_ref[:, 128:] = eye(128).astype(f32)
        for b in range(16):
            if b % 4 == 0:
                between(k, b // 4)
            eight_rows(s_ref, 8 * b)
        aug[pl.ds(o, 128), span] = jnp.dot(
            s_ref[:, 128:], aug[pl.ds(o, 128), span], precision=HI, preferred_element_type=f32
        )
        for i in range(1, 4):

            @pl.when(i > k)
            def _():
                lhs = aug[pl.ds(o, 128), i * 128 : (i + 1) * 128]
                update = t_times(lhs, aug[pl.ds(o, 128), span], HI)
                aug[i * 128 : (i + 1) * 128, span] = aug[i * 128 : (i + 1) * 128, span] - update

        return carry

    lax.fori_loop(0, 4, block, 0)


def pick_pivots(scaled, pivot_column, first):
    waves = (first + iota((PANEL, COLS), 1)).astype(f32)
    taken = jnp.sum(jnp.where(pivot_column == waves, 1.0, 0.0), axis=0, keepdims=True)
    in_run = iota((MINE, COLS), 1) // RUN == iota((MINE, COLS), 0)
    one_hot = jnp.where(in_run, jnp.broadcast_to(taken, (MINE, COLS)), 0.0).astype(bf16)
    return jnp.dot(one_hot, scaled, preferred_element_type=f32).astype(bf16)


class Gather:
    def __init__(self, sems, place):
        self.sems, self.place = sems, place
        y, c, x, z = place
        self.right_x, self.left_x = self.to_x(1), self.to_x(NX - 1)
        self.right_z, self.left_z = self.to_z(1), self.to_z(NZ - 1)

    def to_x(self, d):
        y, c, x, z = self.place
        return (y, c, lax.rem(x + d, NX), z)

    def to_z(self, d):
        y, c, x, z = self.place
        return (y, c, x, lax.rem(z + d, NZ))

    def z_at(self, j):
        z = self.place[3]
        return lax.rem(z + (NZ - j if j <= 4 else j - 4), NZ)

    def x_at(self, i):
        return lax.rem(self.place[2] + (0, NX - 1, 1, 2)[i], NX)

    def copy(self, ref, k, device):
        send, recv = self.sems
        return pltpu.make_async_remote_copy(ref, ref, send.at[k], recv.at[k], device, MESH_ID)

    def run(self, first, last=None):
        for core in range(2):

            @pl.when(self.place[1] == core)
            def _():
                self.process(self.events(core)[first : first + 1 if last is None else last])

    def process(self, events):
        for waits, sends, passes in events:
            for ref, k in waits:
                self.copy(ref, k, self.right_x).wait_recv()
            for ref, k, device in sends:
                self.copy(ref, k, device).start()
            for line in passes:
                self.line(*line).start()

    def run_core(self, core, first, last):
        if first < last:

            @pl.when(self.place[1] == core)
            def _():
                self.process(self.events(core)[first:last])

    def drain(self):
        for core in range(2):

            @pl.when(self.place[1] == core)
            def _():
                for waits, sends, passes in self.events(core):
                    for ref, k, device in sends:
                        self.copy(ref, k, device).wait_send()
                    for line in passes:
                        self.line(*line).wait_send()


class PivotGather(Gather):
    def __init__(self, q_ref, sems, pass_sems, place):
        super().__init__(sems, place)
        self.q_ref, self.pass_sems = q_ref, pass_sems

    def at(self, xs, z=None, core=None, rows=None):
        if z is not None:
            rows = pl.ds(pl.multiple_of(z * MINE, MINE), MINE)
        return self.q_ref.at[self.place[1] if core is None else core, xs, slice(None) if rows is None else rows, :]

    def passed(self, ref, k):
        send, recv = self.pass_sems
        y, c, x, z = self.place
        return pltpu.make_async_remote_copy(ref, ref, send.at[k], recv.at[k], (y, 1 - c, x, z), MESH_ID)

    def line(self, core, i, back=False):
        owner = 1 - self.place[1] if back else self.place[1]
        return self.passed(self.at(i, core=owner) if core == 0 else self.at(slice(None), i, core=owner), i)

    def wait_passed(self):
        for core in range(2):

            @pl.when(self.place[1] == core)
            def _():
                def step(i, carry):
                    self.line(1 - core, i, True).wait_recv()
                    return carry

                lax.fori_loop(0, NZ if core == 0 else NX, step, 0)

    def events(self, core):
        x, z = self.place[2:]
        everything = slice(None)
        if core == 0:
            start = [(self.at(x, z), d, self.to_z(d)) for d in (4, 3, 5, 2, 6, 1, 7)]
            arrive = [(self.at(x, lax.rem(z + NZ - d, NZ)), d) for d in range(1, NZ)]
            mine, a, b, o = (self.x_at(i) for i in range(4))
            whole = [(self.at(mine), 8, self.right_x), (self.at(mine), 9, self.left_x)]
            low, high = pl.ds(0, 64), pl.ds(64, 64)
            first = ([(self.at(a), 8)], [(self.at(a, rows=low), 10, self.right_x)], [(0, a)])
            second = ([(self.at(b), 9)], [(self.at(b, rows=high), 11, self.left_x)], [(0, b)])
            both = [(self.at(o, rows=low), 10), (self.at(o, rows=high), 11)]
            none = ([], [], [])
            return [([], start, []), none, none, (arrive, whole, [(0, mine)]), none, first, second, none, (both, [], [(0, o)])]

        def part(zz, m):
            return self.at(pl.ds(2 * m, 2), zz)

        def key(step, m, side):
            return 4 + 4 * (step - 1) + 2 * m + side

        def onward(step, zz, m):
            out = []
            if step < 4 or m == 0:
                out.append((part(zz[0], m), key(step, m, 0), self.right_z))
            if step < 4 or m == 1:
                out.append((part(zz[1], m), key(step, m, 1), self.left_z))
            return out

        start = [(self.at(x, z), d, self.to_x(d)) for d in (2, 1, 3)]
        arrive = [(self.at(lax.rem(x + NX - d, NX), z), d) for d in range(1, NX)]
        out = [([], start, []), (arrive, onward(1, (z, z), 0) + onward(1, (z, z), 1), [(1, z)])]
        for step in (1, 2, 3):
            zz = self.z_at(step), self.z_at(step + 4)
            for m in range(2):
                waits = [(part(zz[side], m), key(step, m, side)) for side in range(2)]
                out.append((waits, onward(step + 1, zz, m), [(1, zz[side]) for side in range(2)] if m else []))
        far = self.z_at(4)
        out.append(([(part(far, 0), key(4, 0, 0)), (part(far, 1), key(4, 1, 1))], [], [(1, far)]))
        return out


class RowGather(Gather):
    RIGHT = ((1, 0), (2, 0), (1, 1), (1, 2), (1, 3), (3, 0), (2, 1), (2, 2), (2, 3), (4, 0), (3, 1), (3, 2), (3, 3), (4, 1))
    LEFT = ((1, 0), (2, 0), (1, 1), (1, 2), (1, 3), (3, 0), (2, 1), (2, 2), (2, 3), (3, 1), (3, 2), (4, 2), (3, 3), (4, 3))

    def __init__(self, slot, sems, place):
        super().__init__(sems, place)
        self.slot = slot

    def events(self, core):
        x, z = self.place[2:]
        slot = self.slot
        out = []
        if core == 0:
            own = [(slot(x, z), 1, self.right_z), (slot(x, z), 5, self.left_z)]
            own += [(slot(x, z), 8, self.right_x), (slot(x, z), 16, self.left_x)]
            out.append(([], own, []))
            order = (0, 1, 5, 2, 6, 3, 7, 4)

            def along_z(j):
                here = slot(x, self.z_at(j))
                waits, sends = [(here, j)], []
                if j == 4:
                    waits = [(slot(x, self.z_at(4), 0), 4), (slot(x, self.z_at(4), 1), 32)]
                elif j == 3:
                    sends = [(slot(x, self.z_at(3), 0), 4, self.right_z)]
                elif j == 7:
                    sends = [(slot(x, self.z_at(7), 1), 32, self.left_z)]
                else:
                    sends = [(here, j + 1, self.right_z if j < 4 else self.left_z)]
                return waits, sends + [(here, 8 + j, self.right_x), (here, 16 + j, self.left_x)], []

            def along_x(p, side):
                j = order[p]
                here = slot(self.x_at(1 + side), self.z_at(j) if j else z)
                sends = [(here, 24 + j, self.left_x if side else self.right_x)] if p % 2 == side else []
                return [(here, (16 if side else 8) + j)], sends, []

            def opposite(p):
                j = order[p]
                return [(slot(self.x_at(3), self.z_at(j) if j else z), 24 + j)], [], []

            out += [along_z(1), along_z(5), along_x(0, 0), along_x(0, 1), along_z(2), along_z(6)]
            out += [along_x(1, 0), along_x(1, 1), opposite(0), along_z(3), along_z(7)]
            out += [along_x(2, 0), along_x(2, 1), opposite(1), along_z(4)]
            for p in range(3, 8):
                out += [along_x(p, 0), along_x(p, 1), opposite(p - 1)]
            out.append(opposite(7))
            return out

        def key(step, i, side):
            return 4 + 8 * (step - 1) + 2 * i + side

        def onward(step, i, side, here):
            if step > 4 or (step == 4 and i // 2 != side):
                return []
            return [(here, key(step, i, side), self.left_z if side else self.right_z)]

        def along(step, i, side):
            here = slot(self.x_at(i), self.z_at(step + 4 * side if step < 4 else 4))
            return [(here, key(step, i, side))], onward(step + 1, i, side, here), []

        own = [(slot(x, z), d, self.to_x(d)) for d in (2, 1, 3)]
        out.append(([], own + onward(1, 0, 0, slot(x, z)) + onward(1, 0, 1, slot(x, z)), []))
        right, left = list(self.RIGHT), list(self.LEFT)
        out += [along(*right.pop(0), 0), along(*left.pop(0), 1)]
        for i, d in ((1, 1), (2, 3), (3, 2)):
            here = slot(self.x_at(i), z)
            out.append(([(here, d)], onward(1, i, 0, here) + onward(1, i, 1, here), []))
        while right:
            out += [along(*right.pop(0), 0), along(*left.pop(0), 1)]
        return out


EVENTS = 32


def main_kernel(
    density_in,
    weight_in,
    coulomb_in,
    pivots_in,
    dielectric_ref,
    panel_ref,
    q_ref,
    r_ref,
    c_ref,
    qp_ref,
    aug,
    s_ref,
    columns_ref,
    density_ref,
    weight_ref,
    coulomb_ref,
    pivots_ref,
    scaled_ref,
    picked_ref,
    mid_ref,
    local_sem,
    qy_send,
    qy_recv,
    qg_send,
    qg_recv,
    rg_send,
    rg_recv,
    cy_send,
    cy_recv,
    one_send,
    one_recv,
    qx_send,
    qx_recv,
    cx_send,
    cx_recv,
):
    y, c, x, z = (lax.axis_index(a) for a in ("y", "c", "x", "z"))
    place = (y, c, x, z)
    partner = (y, 1 - c, x, z)

    to_y, to_c = 2 * x + z // 4, lax.rem(z // 2, 2)
    mid_x, mid_z = 2 * lax.rem(z, 2) + c, lax.rem(y + 4 * c + 8 - to_y + 4 * (z // 4) + 2 * to_c, NZ)
    middle = (y, to_c, mid_x, mid_z)
    stays = (mid_x == x) & (mid_z == z) & (to_c == c)

    turn = lax.rem(y + 4 * lax.rem(x, 2) + 2 * c + 8 - z, NZ)
    odd = lax.rem(turn, 2)
    origin = (y, lax.rem(x, 2), lax.rem(turn + 3 * odd, 8) // 2, 4 * odd + 2 * c + x // 2)
    last_y = lax.rem(turn + 4 * odd, NY)
    arrives = last_y == y

    def owner_of(xx, zz):
        return lax.rem(zz + y + 16 - 4 * lax.rem(y, 2) - 2 * c + 4 * lax.rem(xx, 2), NY)

    def r_block(pair_core, half, owner):
        return r_ref.at[
            pair_core,
            pl.ds(pl.multiple_of(half * COLS, COLS), COLS),
            pl.ds(pl.multiple_of(owner * OWN, OWN), OWN),
        ]

    def r_slot(xx, zz, part=None):
        first, count = (xx // 2) * COLS, COLS
        if part is not None:
            first, count = first + part * (COLS // 2), COLS // 2
        return r_ref.at[
            lax.rem(xx, 2),
            pl.ds(pl.multiple_of(first, 256), count),
            pl.ds(pl.multiple_of(owner_of(xx, zz) * OWN, OWN), OWN),
        ]

    q_gather = PivotGather(q_ref, (qg_send, qg_recv), (qx_send, qx_recv), place)
    r_gather = RowGather(r_slot, (rg_send, rg_recv), place)

    barrier = pltpu.get_barrier_semaphore()
    greeted = [(lax.rem(y + d, NY), c, x, z) for d in range(1, NY)]
    greeted += [(y, c, x, lax.rem(z + d, NZ)) for d in range(1, NZ)]
    greeted += [(y, c, lax.rem(x + d, NX), z) for d in range(1, NX)]
    greeted += [partner, middle, origin]
    for device in greeted:
        pl.semaphore_signal(barrier, 1, device_id=device, device_id_type=MESH_ID)

    inputs = [
        pltpu.make_async_copy(density_in, density_ref, local_sem.at[0]),
        pltpu.make_async_copy(weight_in, weight_ref, local_sem.at[1]),
        pltpu.make_async_copy(pivots_in, pivots_ref, local_sem.at[2]),
        pltpu.make_async_copy(coulomb_in, coulomb_ref, local_sem.at[3]),
    ]
    for copy in inputs:
        copy.start()
    for copy in inputs:
        copy.wait()
    pivot_row = jnp.concatenate([pivots_ref[i : i + 1, :] for i in range(4)], axis=1)
    first_col = (x * NZ + z) * COLS
    scaled = (density_ref[...].astype(f32) * jnp.sqrt(weight_ref[...])).astype(bf16)
    picked_own = pick_pivots(scaled, column_of(pivot_row.astype(f32)), first_col)
    own_rows = pl.ds(pl.multiple_of(z * MINE, MINE), MINE)
    own_pairs = pl.ds(pl.multiple_of(y * OWN, OWN), OWN)
    scaled_ref[...] = scaled
    picked_ref[...] = picked_own
    c_ref[c, :, own_pairs] = scaled
    q_ref[c, x, own_rows, own_pairs] = picked_own
    own_q = q_ref.at[c, x, own_rows, own_pairs]
    pl.semaphore_wait(barrier, len(greeted))

    def picked_copy(d):
        peer = (lax.rem(y + d, NY), c, x, z)
        return pltpu.make_async_remote_copy(
            picked_ref, own_q, qy_send.at[d], qy_recv.at[d], peer, MESH_ID
        )

    def picked_arrival(d):
        other = lax.rem(y + NY - d, NY)
        there = q_ref.at[c, x, own_rows, pl.ds(pl.multiple_of(other * OWN, OWN), OWN)]
        return pltpu.make_async_remote_copy(
            there, there, qy_send.at[d], qy_recv.at[d], partner, MESH_ID
        )

    for d in (4, 3, 5, 2, 6, 1, 7):
        picked_copy(d).start()

    away = pltpu.make_async_remote_copy(scaled_ref, mid_ref, one_send.at[0], one_recv.at[0], middle, MESH_ID)
    stay = pltpu.make_async_copy(scaled_ref, mid_ref, local_sem.at[0])
    here = r_slot(x, z)
    there = r_block(lax.rem(x, 2), x // 2, y)
    onward = pltpu.make_async_remote_copy(mid_ref, there, one_send.at[1], one_recv.at[1], (last_y, c, x, z), MESH_ID)
    onward_in = pltpu.make_async_remote_copy(here, here, one_send.at[1], one_recv.at[1], partner, MESH_ID)
    keep = pltpu.make_async_copy(mid_ref, here, local_sem.at[1])

    def either(condition, yes, no):
        pl.when(condition)(yes)
        pl.when(jnp.logical_not(condition))(no)

    def second_move():
        either(stays, stay.wait, away.wait_recv)
        either(arrives, keep.start, onward.start)

    def c_of(owner):
        return c_ref.at[c, :, pl.ds(pl.multiple_of(owner * OWN, OWN), OWN)]

    def ring_y(step):
        up, down = (lax.rem(y + 1, NY), c, x, z), (lax.rem(y + NY - 1, NY), c, x, z)
        k = 2 * (step - 1)
        out = [(c_of(lax.rem(y + NY - step + 1, NY)), c_of(lax.rem(y + NY - step, NY)), k, up)]
        if step < 4:
            out.append((c_of(lax.rem(y + step - 1, NY)), c_of(lax.rem(y + step, NY)), k + 1, down))
        return out

    def c_copies(step, received):
        for sent, came, k, device in ring_y(step):
            ref = came if received else sent
            yield pltpu.make_async_remote_copy(ref, ref, cy_send.at[k], cy_recv.at[k], device, MESH_ID)

    def c_pass(owner, back=False):
        ref = c_ref.at[1 - c if back else c, :, pl.ds(pl.multiple_of(owner * OWN, OWN), OWN)]
        return pltpu.make_async_remote_copy(ref, ref, cx_send.at[owner], cx_recv.at[owner], partner, MESH_ID)

    def c_advance(event):
        if event > 1:
            for copy in c_copies(event - 1, True):
                copy.wait_recv()
            for away in (NY - event + 1, event - 1)[: 2 if event < 5 else 1]:
                c_pass(lax.rem(y + away, NY)).start()
        if event < 5:
            for copy in c_copies(event, False):
                copy.start()

    def repeat(count, do):
        def step(i, carry):
            do(i)
            return carry

        lax.fori_loop(0, count, step, 0)

    either(stays, stay.start, away.start)
    c_pass(y).start()
    c_advance(1)

    run_column = column_of((pivot_row // RUN).astype(f32))
    high_column = column_of((pivot_row // 128).astype(f32))
    low_column = column_of((pivot_row % 128).astype(f32))
    in_row = (high_column == iota((PANEL, 128), 1).astype(f32)).astype(f32)
    picked = jnp.dot(in_row, coulomb_ref[...], precision=HI, preferred_element_type=f32)
    at_lane = low_column == iota((PANEL, 128), 1).astype(f32)
    pivot_scale = jnp.sqrt(jnp.sum(jnp.where(at_lane, picked, 0.0), axis=1, keepdims=True))
    pivot_scale_row = row_of(pivot_scale)
    order = (run_column == iota((PANEL, PANEL), 1).astype(f32)).astype(bf16)

    for d in range(1, NY):
        picked_arrival(d).wait_recv()
    q_gather.run(0)
    c_advance(2)
    q_gather.run(1)
    second_move()
    q_gather.run(2, 4)
    c_advance(3)
    q_gather.run(4)
    either(arrives, keep.wait, onward_in.wait_recv)
    r_gather.run(0)
    q_gather.run(5, 7)
    c_advance(4)
    r_gather.run(1, 3)
    q_gather.run(7, 9)
    q_gather.wait_passed()

    gram = None
    for h in range(2):
        qp_ref[h] = jnp.dot(
            order, q_ref[h].reshape(PANEL, HALF), preferred_element_type=f32
        ).astype(bf16)
        part = times_t(qp_ref[h], qp_ref[h])
        gram = part if gram is None else gram + part
    unit = eye(PANEL).astype(f32)
    aug[:, :PANEL] = pivot_scale * pivot_scale_row * gram + unit
    aug[:, PANEL:] = unit
    r_gather.run(3, 7)
    c_advance(5)

    def between(k, part):
        for block in range(4):

            @pl.when(k == block)
            def _():
                r_gather.run(7 + 4 * block + part)

    factor_and_inverse(aug, s_ref, between)

    diag = jnp.concatenate(
        [
            jnp.sum(jnp.where(eye(128), aug[i : i + 128, i : i + 128], 0.0), axis=1, keepdims=True)
            for i in range(0, PANEL, 128)
        ],
        axis=0,
    )
    aug[:, PANEL:] = aug[:, PANEL:] / diag

    runs = ROWS // RUN
    run_row = pivot_row // RUN
    pick = (run_row == (y * NC + c) * runs + iota((runs, PANEL), 0)).astype(f32)
    top = None
    for part in split3(aug[:, :PANEL]):
        rows = jnp.dot(pick.astype(bf16), part.astype(bf16), preferred_element_type=f32)
        top = rows if top is None else top + rows
    top = top * jnp.sum(pick * row_of(diag), axis=1, keepdims=True)
    position = jnp.sum(pick * iota((runs, PANEL), 1).astype(f32), axis=1, keepdims=True)
    within = jnp.sum(pick * (pivot_row % RUN).astype(f32), axis=1, keepdims=True)

    repeat(NY, lambda i: c_pass(i, True).wait_recv())

    first_row = (y * NC + c) * ROWS
    row_scale = jnp.sqrt(column_of(lanes_of(coulomb_ref, (y * NC + c) * 8, 8)))
    col_scale = jnp.sqrt(lanes_of(coulomb_ref, (x * NZ + z) * 4, 4))
    tile = 256

    def product(ref, rows, wanted):
        parts = []
        for j in wanted:
            zz = r_gather.z_at(j) if j else z
            for xx in range(2):
                owner = pl.multiple_of(owner_of(xx, zz) * OWN, OWN)
                parts.append(ref[xx, rows, pl.ds(owner, OWN)])
        return jnp.concatenate(parts, axis=1)

    done = [23, 23]
    groups = ((0, 1, 5, 2), (6, 3), (7, 4))
    ready = {0: (21, 27, 31), 1: (20, 28, 31)}
    for g, wanted in enumerate(groups):
        for core in range(2):
            r_gather.run_core(core, done[core], ready[core][g] + 1)
            done[core] = max(done[core], ready[core][g] + 1)
        everything = slice(None)
        c_part, q_part = product(c_ref, everything, wanted), product(qp_ref, everything, wanted)
        for t in range(ROWS // tile):
            rows = slice(t * tile, (t + 1) * tile)
            r_part = product(r_ref, rows, wanted)
            gram, columns = times_t(r_part, c_part), times_t(r_part, q_part)
            if g == 0:
                dielectric_ref[rows, :], panel_ref[rows, :] = gram, columns
                continue
            gram, columns = dielectric_ref[rows, :] + gram, panel_ref[rows, :] + columns
            if g < len(groups) - 1:
                dielectric_ref[rows, :], panel_ref[rows, :] = gram, columns
                continue
            scale = row_scale[rows]
            numbers = first_row + t * tile + iota((tile, COLS), 0)
            same = numbers == first_col + iota((tile, COLS), 1)
            dielectric_ref[rows, :] = scale * col_scale * gram + jnp.where(same, 1.0, 0.0)
            same = numbers == pivot_row
            columns_ref[...] = scale * pivot_scale_row * columns + jnp.where(same, 1.0, 0.0)
            panel_ref[rows, :256] = times_t(columns_ref[:, :256], aug[:256, PANEL : PANEL + 256], HI)
            panel_ref[rows, 256:] = times_t(columns_ref[...], aug[256:, PANEL:], HI)

    lane = iota((RUN, PANEL), 1).astype(f32)
    line = iota((RUN, PANEL), 0).astype(f32)
    for q in range(runs):
        rows = slice(q * RUN, (q + 1) * RUN)
        over = (line == within[q : q + 1]) & (lane >= position[q : q + 1])
        panel_ref[rows, :] = jnp.where(over, jnp.broadcast_to(top[q : q + 1, :], (RUN, PANEL)), panel_ref[rows, :])

    for d in range(1, NY):
        picked_copy(d).wait_send()

    @pl.when(jnp.logical_not(stays))
    def _():
        away.wait_send()

    @pl.when(jnp.logical_not(arrives))
    def _():
        onward.wait_send()

    for step in range(1, 5):
        for copy in c_copies(step, False):
            copy.wait_send()
    repeat(NY, lambda i: c_pass(i).wait_send())
    q_gather.drain()
    r_gather.drain()


def body(pair_density, pair_weight, coulomb, pivot_rows):
    vmem = pl.BlockSpec(memory_space=pltpu.VMEM)
    dma = pltpu.SemaphoreType.DMA
    return pl.pallas_call(
        main_kernel,
        out_shape=(
            jax.ShapeDtypeStruct((ROWS, COLS), f32),
            jax.ShapeDtypeStruct((ROWS, PANEL), f32),
        ),
        in_specs=[pl.BlockSpec(memory_space=pl.ANY)] * 4,
        out_specs=(vmem, vmem),
        scratch_shapes=[
            pltpu.VMEM((2, NX, NZ * MINE, HALF), bf16),
            pltpu.VMEM((2, ROWS, HALF), bf16),
            pltpu.VMEM((2, COLS, HALF), bf16),
            pltpu.VMEM((2, PANEL, HALF), bf16),
            pltpu.VMEM((PANEL, 2 * PANEL), f32),
            pltpu.VMEM((128, 256), f32),
            pltpu.VMEM((256, PANEL), f32),
            pltpu.VMEM((COLS, OWN), bf16),
            pltpu.VMEM((1, OWN), f32),
            pltpu.VMEM((128, 128), f32),
            pltpu.VMEM((4, 128), jnp.int32),
            pltpu.VMEM((COLS, OWN), bf16),
            pltpu.VMEM((MINE, OWN), bf16),
            pltpu.VMEM((COLS, OWN), bf16),
            dma((4,)),
            dma((NY,)),
            dma((NY,)),
            dma((20,)),
            dma((20,)),
            dma((36,)),
            dma((36,)),
            dma((7,)),
            dma((7,)),
            dma((2,)),
            dma((2,)),
            dma((NZ,)),
            dma((NZ,)),
            dma((NY,)),
            dma((NY,)),
        ],
        compiler_params=pltpu.CompilerParams(
            collective_id=0, has_side_effects=True, vmem_limit_bytes=40 * 2**20
        ),
        name="gather_factor_panel",
    )(pair_density, pair_weight.reshape(1, OWN), coulomb.reshape(128, 128), pivot_rows.reshape(4, 128))


def solution(mesh):
    finer = Mesh(mesh.devices.reshape(NY, NC, NX, NZ), ("y", "c", "x", "z"))
    return jax.shard_map(
        body,
        mesh=finer,
        in_specs=(P(("x", "z"), ("y", "c")), P(("y", "c")), P(), P()),
        out_specs=(P(("y", "c"), ("x", "z")), P(("y", "c"), None)),
        check_vma=False,
    )
```

```python
import functools

import jax
import jax.numpy as jnp
from jax import lax
from jax.experimental import pallas as pl
from jax.experimental.pallas import tpu as pltpu
from jax.sharding import Mesh
from jax.sharding import PartitionSpec as P

NG = 16384
PANEL = 512
RUN = NG // PANEL
NY, NC, NX, NZ = 8, 2, 4, 8
COLS = NG // (NX * NZ)
ROWS = NG // (NY * NC)
OWN = 128
HALF = NY * OWN
MINE = COLS // RUN
HI = lax.Precision.HIGHEST
f32, bf16 = jnp.float32, jnp.bfloat16
MESH_ID = pl.DeviceIdType.MESH


def iota(shape, dim):
    return lax.broadcasted_iota(jnp.int32, shape, dim)


def eye(n):
    return iota((n, n), 0) == iota((n, n), 1)


def column_of(row):
    blocks = []
    for i in range(row.shape[1] // 128):
        part = jnp.broadcast_to(row[:, i * 128 : (i + 1) * 128], (128, 128))
        blocks.append(jnp.sum(jnp.where(eye(128), part, 0.0), axis=1, keepdims=True))
    return jnp.concatenate(blocks, axis=0)


def row_of(column):
    blocks = []
    for i in range(column.shape[0] // 128):
        part = jnp.broadcast_to(column[i * 128 : (i + 1) * 128], (128, 128))
        blocks.append(jnp.sum(jnp.where(eye(128), part, 0.0), axis=0, keepdims=True))
    return jnp.concatenate(blocks, axis=1)


def lanes_of(ref, first, count):
    return jnp.concatenate([ref[pl.ds(first + i, 1), :] for i in range(count)], axis=1)


def times_t(a, b, precision=None):
    return lax.dot_general(
        a, b, (((1,), (1,)), ((), ())), precision=precision, preferred_element_type=f32
    )


def t_times(a, b, precision=None):
    return lax.dot_general(
        a, b, (((0,), (0,)), ((), ())), precision=precision, preferred_element_type=f32
    )


def split3(y):
    high = y.astype(bf16).astype(f32)
    rest = y - high
    middle = rest.astype(bf16).astype(f32)
    return high, middle, rest - middle


def eight_rows(s_ref, c):
    sub = iota((8, 128), 0)

    def taken(first):
        rows = s_ref[first : first + 8, :]
        cols = [jnp.broadcast_to(rows[:, c + j : c + j + 1], (8, 128)) for j in range(8)]
        return [cols, rows[:, :128], rows[:, 128:]]

    ahead = [first for first in (c + 8, c + 16) if first < 128]
    cols, left, right = taken(c)
    later = [taken(first) for first in ahead]
    for j in range(8):
        r = lax.rsqrt(jnp.broadcast_to(cols[j][j : j + 1, :], (8, 128)))
        f = jnp.where(sub > j, cols[j] * r, 0.0)
        own = jnp.where(sub == j, r, 1.0)
        factors = [part[0][j] * r for part in later]
        for m in range(j + 1, 8):
            pivot = jnp.broadcast_to(cols[m][j : j + 1, :], (8, 128)) * r
            cols[m] = cols[m] - f * pivot
            for part, g in zip(later, factors):
                part[0][m] = part[0][m] - g * pivot
        left_j = jnp.broadcast_to(left[j : j + 1, :], (8, 128)) * r
        right_j = jnp.broadcast_to(right[j : j + 1, :], (8, 128)) * r
        left = left * own - f * left_j
        right = right * own - f * right_j
        for part, g in zip(later, factors):
            part[1] = part[1] - g * left_j
            part[2] = part[2] - g * right_j
    y = jnp.concatenate([left, right], axis=1)
    s_ref[c : c + 8, :] = y
    for first, part in zip(ahead, later):
        s_ref[first : first + 8, :] = jnp.concatenate(part[1:], axis=1)
    rest = c + 24
    if rest < 128:
        h, m, l = split3(y)
        lhs = jnp.concatenate([h, h, m, h, l, m], axis=0)[:, :128].astype(bf16)
        rhs = jnp.concatenate([h, m, h, l, h, m], axis=0).astype(bf16)
        s_ref[rest:, :] = s_ref[rest:, :] - t_times(lhs, rhs)[rest:, :]


def factor_and_inverse(aug, s_ref, between):
    def block(k, carry):
        o = pl.multiple_of(k * 128, 128)
        span = pl.ds(o, PANEL + 128)
        s_ref[:, :128] = aug[pl.ds(o, 128), pl.ds(o, 128)]
        s_ref[:, 128:] = eye(128).astype(f32)
        for b in range(16):
            if b % 4 == 0:
                between(k, b // 4)
            eight_rows(s_ref, 8 * b)
        aug[pl.ds(o, 128), span] = jnp.dot(
            s_ref[:, 128:], aug[pl.ds(o, 128), span], precision=HI, preferred_element_type=f32
        )
        for i in range(1, 4):

            @pl.when(i > k)
            def _():
                lhs = aug[pl.ds(o, 128), i * 128 : (i + 1) * 128]
                update = t_times(lhs, aug[pl.ds(o, 128), span], HI)
                aug[i * 128 : (i + 1) * 128, span] = aug[i * 128 : (i + 1) * 128, span] - update

        return carry

    lax.fori_loop(0, 4, block, 0)


def pick_pivots(scaled, pivot_column, first):
    waves = (first + iota((PANEL, COLS), 1)).astype(f32)
    taken = jnp.sum(jnp.where(pivot_column == waves, 1.0, 0.0), axis=0, keepdims=True)
    in_run = iota((MINE, COLS), 1) // RUN == iota((MINE, COLS), 0)
    one_hot = jnp.where(in_run, jnp.broadcast_to(taken, (MINE, COLS)), 0.0).astype(bf16)
    return jnp.dot(one_hot, scaled, preferred_element_type=f32).astype(bf16)


class Gather:
    def __init__(self, sems, place):
        self.sems, self.place = sems, place
        y, c, x, z = place
        self.right_x, self.left_x = self.to_x(1), self.to_x(NX - 1)
        self.right_z, self.left_z = self.to_z(1), self.to_z(NZ - 1)

    def to_x(self, d):
        y, c, x, z = self.place
        return (y, c, lax.rem(x + d, NX), z)

    def to_z(self, d):
        y, c, x, z = self.place
        return (y, c, x, lax.rem(z + d, NZ))

    def z_at(self, j):
        z = self.place[3]
        return lax.rem(z + (NZ - j if j <= 4 else j - 4), NZ)

    def x_at(self, i):
        return lax.rem(self.place[2] + (0, NX - 1, 1, 2)[i], NX)

    def copy(self, ref, k, device):
        send, recv = self.sems
        return pltpu.make_async_remote_copy(ref, ref, send.at[k], recv.at[k], device, MESH_ID)

    def run(self, first, last=None):
        for core in range(2):

            @pl.when(self.place[1] == core)
            def _():
                self.process(self.events(core)[first : first + 1 if last is None else last])

    def process(self, events):
        for waits, sends, passes in events:
            for ref, k in waits:
                self.copy(ref, k, self.right_x).wait_recv()
            for ref, k, device in sends:
                self.copy(ref, k, device).start()
            for line in passes:
                self.line(*line).start()

    def run_core(self, core, first, last):
        if first < last:

            @pl.when(self.place[1] == core)
            def _():
                self.process(self.events(core)[first:last])

    def drain(self):
        for core in range(2):

            @pl.when(self.place[1] == core)
            def _():
                for waits, sends, passes in self.events(core):
                    for ref, k, device in sends:
                        self.copy(ref, k, device).wait_send()
                    for line in passes:
                        self.line(*line).wait_send()


class PivotGather(Gather):
    def __init__(self, q_ref, sems, pass_sems, place):
        super().__init__(sems, place)
        self.q_ref, self.pass_sems = q_ref, pass_sems

    def at(self, xs, z=None, core=None, rows=None):
        if z is not None:
            rows = pl.ds(pl.multiple_of(z * MINE, MINE), MINE)
        return self.q_ref.at[self.place[1] if core is None else core, xs, slice(None) if rows is None else rows, :]

    def passed(self, ref, k):
        send, recv = self.pass_sems
        y, c, x, z = self.place
        return pltpu.make_async_remote_copy(ref, ref, send.at[k], recv.at[k], (y, 1 - c, x, z), MESH_ID)

    def line(self, core, i, back=False):
        owner = 1 - self.place[1] if back else self.place[1]
        return self.passed(self.at(i, core=owner) if core == 0 else self.at(slice(None), i, core=owner), i)

    def wait_passed(self):
        for core in range(2):

            @pl.when(self.place[1] == core)
            def _():
                def step(i, carry):
                    self.line(1 - core, i, True).wait_recv()
                    return carry

                lax.fori_loop(0, NZ if core == 0 else NX, step, 0)

    def events(self, core):
        x, z = self.place[2:]
        everything = slice(None)
        if core == 0:
            start = [(self.at(x, z), d, self.to_z(d)) for d in (4, 3, 5, 2, 6, 1, 7)]
            arrive = [(self.at(x, lax.rem(z + NZ - d, NZ)), d) for d in range(1, NZ)]
            mine, a, b, o = (self.x_at(i) for i in range(4))
            whole = [(self.at(mine), 8, self.right_x), (self.at(mine), 9, self.left_x)]
            low, high = pl.ds(0, 64), pl.ds(64, 64)
            first = ([(self.at(a), 8)], [(self.at(a, rows=low), 10, self.right_x)], [(0, a)])
            second = ([(self.at(b), 9)], [(self.at(b, rows=high), 11, self.left_x)], [(0, b)])
            both = [(self.at(o, rows=low), 10), (self.at(o, rows=high), 11)]
            none = ([], [], [])
            return [([], start, []), none, none, (arrive, whole, [(0, mine)]), none, first, second, none, (both, [], [(0, o)])]

        def part(zz, m):
            return self.at(pl.ds(2 * m, 2), zz)

        def key(step, m, side):
            return 4 + 4 * (step - 1) + 2 * m + side

        def onward(step, zz, m):
            out = []
            if step < 4 or m == 0:
                out.append((part(zz[0], m), key(step, m, 0), self.right_z))
            if step < 4 or m == 1:
                out.append((part(zz[1], m), key(step, m, 1), self.left_z))
            return out

        start = [(self.at(x, z), d, self.to_x(d)) for d in (2, 1, 3)]
        arrive = [(self.at(lax.rem(x + NX - d, NX), z), d) for d in range(1, NX)]
        out = [([], start, []), (arrive, onward(1, (z, z), 0) + onward(1, (z, z), 1), [(1, z)])]
        for step in (1, 2, 3):
            zz = self.z_at(step), self.z_at(step + 4)
            for m in range(2):
                waits = [(part(zz[side], m), key(step, m, side)) for side in range(2)]
                out.append((waits, onward(step + 1, zz, m), [(1, zz[side]) for side in range(2)] if m else []))
        far = self.z_at(4)
        out.append(([(part(far, 0), key(4, 0, 0)), (part(far, 1), key(4, 1, 1))], [], [(1, far)]))
        return out


class RowGather(Gather):
    RIGHT = ((1, 0), (2, 0), (1, 1), (1, 2), (1, 3), (3, 0), (2, 1), (2, 2), (2, 3), (4, 0), (3, 1), (3, 2), (3, 3), (4, 1))
    LEFT = ((1, 0), (2, 0), (1, 1), (1, 2), (1, 3), (3, 0), (2, 1), (2, 2), (2, 3), (3, 1), (3, 2), (4, 2), (3, 3), (4, 3))

    def __init__(self, slot, sems, place):
        super().__init__(sems, place)
        self.slot = slot

    def events(self, core):
        x, z = self.place[2:]
        slot = self.slot
        out = []
        if core == 0:
            own = [(slot(x, z), 1, self.right_z), (slot(x, z), 5, self.left_z)]
            own += [(slot(x, z), 8, self.right_x), (slot(x, z), 16, self.left_x)]
            out.append(([], own, []))
            order = (0, 1, 5, 2, 6, 3, 7, 4)

            def along_z(j):
                here = slot(x, self.z_at(j))
                waits, sends = [(here, j)], []
                if j == 4:
                    waits = [(slot(x, self.z_at(4), 0), 4), (slot(x, self.z_at(4), 1), 32)]
                elif j == 3:
                    sends = [(slot(x, self.z_at(3), 0), 4, self.right_z)]
                elif j == 7:
                    sends = [(slot(x, self.z_at(7), 1), 32, self.left_z)]
                else:
                    sends = [(here, j + 1, self.right_z if j < 4 else self.left_z)]
                return waits, sends + [(here, 8 + j, self.right_x), (here, 16 + j, self.left_x)], []

            def along_x(p, side):
                j = order[p]
                here = slot(self.x_at(1 + side), self.z_at(j) if j else z)
                sends = [(here, 24 + j, self.left_x if side else self.right_x)] if p % 2 == side else []
                return [(here, (16 if side else 8) + j)], sends, []

            def opposite(p):
                j = order[p]
                return [(slot(self.x_at(3), self.z_at(j) if j else z), 24 + j)], [], []

            out += [along_z(1), along_z(5), along_x(0, 0), along_x(0, 1), along_z(2), along_z(6)]
            out += [along_x(1, 0), along_x(1, 1), opposite(0), along_z(3), along_z(7)]
            out += [along_x(2, 0), along_x(2, 1), opposite(1), along_z(4)]
            for p in range(3, 8):
                out += [along_x(p, 0), along_x(p, 1), opposite(p - 1)]
            out.append(opposite(7))
            return out

        def key(step, i, side):
            return 4 + 8 * (step - 1) + 2 * i + side

        def onward(step, i, side, here):
            if step > 4 or (step == 4 and i // 2 != side):
                return []
            return [(here, key(step, i, side), self.left_z if side else self.right_z)]

        def along(step, i, side):
            here = slot(self.x_at(i), self.z_at(step + 4 * side if step < 4 else 4))
            return [(here, key(step, i, side))], onward(step + 1, i, side, here), []

        own = [(slot(x, z), d, self.to_x(d)) for d in (2, 1, 3)]
        out.append(([], own + onward(1, 0, 0, slot(x, z)) + onward(1, 0, 1, slot(x, z)), []))
        right, left = list(self.RIGHT), list(self.LEFT)
        out += [along(*right.pop(0), 0), along(*left.pop(0), 1)]
        for i, d in ((1, 1), (2, 3), (3, 2)):
            here = slot(self.x_at(i), z)
            out.append(([(here, d)], onward(1, i, 0, here) + onward(1, i, 1, here), []))
        while right:
            out += [along(*right.pop(0), 0), along(*left.pop(0), 1)]
        return out


EVENTS = 32


def main_kernel(
    density_in,
    weight_in,
    coulomb_in,
    pivots_in,
    dielectric_ref,
    panel_ref,
    q_ref,
    r_ref,
    c_ref,
    qp_ref,
    aug,
    s_ref,
    columns_ref,
    density_ref,
    weight_ref,
    coulomb_ref,
    pivots_ref,
    scaled_ref,
    picked_ref,
    mid_ref,
    direct_ref,
    local_sem,
    qy_send,
    qy_recv,
    qg_send,
    qg_recv,
    rg_send,
    rg_recv,
    cy_send,
    cy_recv,
    one_send,
    one_recv,
    qx_send,
    qx_recv,
    cx_send,
    cx_recv,
):
    y, c, x, z = (lax.axis_index(a) for a in ("y", "c", "x", "z"))
    place = (y, c, x, z)
    partner = (y, 1 - c, x, z)

    to_y, to_c = 2 * x + z // 4, lax.rem(z // 2, 2)
    mid_x, mid_z = 2 * lax.rem(z, 2) + c, lax.rem(y + 4 * c + 8 - to_y + 4 * (z // 4) + 2 * to_c, NZ)
    middle = (y, to_c, mid_x, mid_z)
    stays = (mid_x == x) & (mid_z == z) & (to_c == c)

    turn = lax.rem(y + 4 * lax.rem(x, 2) + 2 * c + 8 - z, NZ)
    odd = lax.rem(turn, 2)
    origin = (y, lax.rem(x, 2), lax.rem(turn + 3 * odd, 8) // 2, 4 * odd + 2 * c + x // 2)
    last_y = lax.rem(turn + 4 * odd, NY)
    arrives = last_y == y

    def owner_of(xx, zz):
        return lax.rem(zz + y + 16 - 4 * lax.rem(y, 2) - 2 * c + 4 * lax.rem(xx, 2), NY)

    def r_block(pair_core, half, owner):
        return r_ref.at[
            pair_core,
            pl.ds(pl.multiple_of(half * COLS, COLS), COLS),
            pl.ds(pl.multiple_of(owner * OWN, OWN), OWN),
        ]

    def r_slot(xx, zz, part=None):
        first, count = (xx // 2) * COLS, COLS
        if part is not None:
            first, count = first + part * (COLS // 2), COLS // 2
        return r_ref.at[
            lax.rem(xx, 2),
            pl.ds(pl.multiple_of(first, 256), count),
            pl.ds(pl.multiple_of(owner_of(xx, zz) * OWN, OWN), OWN),
        ]

    q_gather = PivotGather(q_ref, (qg_send, qg_recv), (qx_send, qx_recv), place)
    r_gather = RowGather(r_slot, (rg_send, rg_recv), place)

    barrier = pltpu.get_barrier_semaphore()
    greeted = [(lax.rem(y + d, NY), c, x, z) for d in range(1, NY)]
    greeted += [(y, c, x, lax.rem(z + d, NZ)) for d in range(1, NZ)]
    greeted += [(y, c, lax.rem(x + d, NX), z) for d in range(1, NX)]
    greeted += [partner, middle, origin]
    for device in greeted:
        pl.semaphore_signal(barrier, 1, device_id=device, device_id_type=MESH_ID)

    inputs = [
        pltpu.make_async_copy(density_in, density_ref, local_sem.at[0]),
        pltpu.make_async_copy(weight_in, weight_ref, local_sem.at[1]),
        pltpu.make_async_copy(pivots_in, pivots_ref, local_sem.at[2]),
        pltpu.make_async_copy(coulomb_in, coulomb_ref, local_sem.at[3]),
    ]
    for copy in inputs:
        copy.start()
    for copy in inputs:
        copy.wait()
    pivot_row = jnp.concatenate([pivots_ref[i : i + 1, :] for i in range(4)], axis=1)
    first_col = (x * NZ + z) * COLS
    scaled = (density_ref[...].astype(f32) * jnp.sqrt(weight_ref[...])).astype(bf16)
    picked_own = pick_pivots(scaled, column_of(pivot_row.astype(f32)), first_col)
    own_rows = pl.ds(pl.multiple_of(z * MINE, MINE), MINE)
    own_pairs = pl.ds(pl.multiple_of(y * OWN, OWN), OWN)
    scaled_ref[...] = scaled
    picked_ref[...] = picked_own
    c_ref[c, :, own_pairs] = scaled
    q_ref[c, x, own_rows, own_pairs] = picked_own
    own_q = q_ref.at[c, x, own_rows, own_pairs]
    pl.semaphore_wait(barrier, len(greeted))

    def picked_copy(d):
        peer = (lax.rem(y + d, NY), c, x, z)
        return pltpu.make_async_remote_copy(
            picked_ref, own_q, qy_send.at[d], qy_recv.at[d], peer, MESH_ID
        )

    def picked_arrival(d):
        other = lax.rem(y + NY - d, NY)
        there = q_ref.at[c, x, own_rows, pl.ds(pl.multiple_of(other * OWN, OWN), OWN)]
        return pltpu.make_async_remote_copy(
            there, there, qy_send.at[d], qy_recv.at[d], partner, MESH_ID
        )

    for d in (4, 3, 5, 2, 6, 1, 7):
        picked_copy(d).start()

    away = pltpu.make_async_remote_copy(scaled_ref, mid_ref, one_send.at[0], one_recv.at[0], middle, MESH_ID)
    stay = pltpu.make_async_copy(scaled_ref, mid_ref, local_sem.at[0])
    here = r_slot(x, z)
    there = r_block(lax.rem(x, 2), x // 2, y)
    onward = pltpu.make_async_remote_copy(mid_ref, there, one_send.at[1], one_recv.at[1], (last_y, c, x, z), MESH_ID)
    onward_in = pltpu.make_async_remote_copy(here, here, one_send.at[1], one_recv.at[1], partner, MESH_ID)
    keep = pltpu.make_async_copy(mid_ref, here, local_sem.at[1])

    def either(condition, yes, no):
        pl.when(condition)(yes)
        pl.when(jnp.logical_not(condition))(no)

    def second_move():
        either(stays, stay.wait, away.wait_recv)
        either(arrives, keep.start, onward.start)

    def c_of(owner):
        return c_ref.at[c, :, pl.ds(pl.multiple_of(owner * OWN, OWN), OWN)]

    def ring_y(step):
        up, down = (lax.rem(y + 1, NY), c, x, z), (lax.rem(y + NY - 1, NY), c, x, z)
        k = 2 * (step - 1)
        out = [(c_of(lax.rem(y + NY - step + 1, NY)), c_of(lax.rem(y + NY - step, NY)), k, up)]
        if step < 4:
            out.append((c_of(lax.rem(y + step - 1, NY)), c_of(lax.rem(y + step, NY)), k + 1, down))
        return out

    def c_copies(step, received):
        for sent, came, k, device in ring_y(step):
            ref = came if received else sent
            yield pltpu.make_async_remote_copy(ref, ref, cy_send.at[k], cy_recv.at[k], device, MESH_ID)

    def c_pass(owner, back=False):
        ref = c_ref.at[1 - c if back else c, :, pl.ds(pl.multiple_of(owner * OWN, OWN), OWN)]
        return pltpu.make_async_remote_copy(ref, ref, cx_send.at[owner], cx_recv.at[owner], partner, MESH_ID)

    def c_advance(event):
        if event > 1:
            for copy in c_copies(event - 1, True):
                copy.wait_recv()
            for away in (NY - event + 1, event - 1)[: 2 if event < 5 else 1]:
                c_pass(lax.rem(y + away, NY)).start()
        if event < 5:
            for copy in c_copies(event, False):
                copy.start()

    def repeat(count, do):
        def step(i, carry):
            do(i)
            return carry

        lax.fori_loop(0, count, step, 0)

    either(stays, stay.start, away.start)
    run_column = column_of((pivot_row // RUN).astype(f32))
    high_column = column_of((pivot_row // 128).astype(f32))
    low_column = column_of((pivot_row % 128).astype(f32))
    in_row = (high_column == iota((PANEL, 128), 1).astype(f32)).astype(f32)
    picked = jnp.dot(in_row, coulomb_ref[...], precision=HI, preferred_element_type=f32)
    at_lane = low_column == iota((PANEL, 128), 1).astype(f32)
    pivot_scale = jnp.sqrt(jnp.sum(jnp.where(at_lane, picked, 0.0), axis=1, keepdims=True))
    pivot_scale_row = row_of(pivot_scale)
    order = (run_column == iota((PANEL, PANEL), 1).astype(f32)).astype(bf16)

    for d in range(1, NY):
        picked_arrival(d).wait_recv()
    q_gather.run(0, 2)
    second_move()
    c_pass(y).start()
    c_advance(1)
    q_gather.run(2, 4)
    q_gather.run(4)
    either(arrives, keep.wait, onward_in.wait_recv)
    r_gather.run(0)
    q_gather.run(5, 7)
    c_advance(2)
    r_gather.run(1, 3)
    q_gather.run(7, 9)
    q_gather.wait_passed()

    gram = None
    for h in range(2):
        qp_ref[h] = jnp.dot(
            order, q_ref[h].reshape(PANEL, HALF), preferred_element_type=f32
        ).astype(bf16)
        part = times_t(qp_ref[h], qp_ref[h])
        gram = part if gram is None else gram + part
    unit = eye(PANEL).astype(f32)
    aug[:, :PANEL] = pivot_scale * pivot_scale_row * gram + unit
    aug[:, PANEL:] = unit
    r_gather.run(3, 7)
    c_advance(3)

    def between(k, part):
        for block in range(4):
            at = 4 * block + part
            low, high = (7 + (19 * i) // 16 for i in (at, at + 1))
            if low < high or at in (4, 8):

                @pl.when(k == block)
                def _():
                    r_gather.run(low, high)
                    if at == 4:
                        c_advance(4)
                    if at == 8:
                        c_advance(5)

    factor_and_inverse(aug, s_ref, between)

    diag = jnp.concatenate(
        [
            jnp.sum(jnp.where(eye(128), aug[i : i + 128, i : i + 128], 0.0), axis=1, keepdims=True)
            for i in range(0, PANEL, 128)
        ],
        axis=0,
    )
    aug[:, PANEL:] = aug[:, PANEL:] / diag

    runs = ROWS // RUN
    run_row = pivot_row // RUN
    pick = (run_row == (y * NC + c) * runs + iota((runs, PANEL), 0)).astype(f32)
    top = None
    for part in split3(aug[:, :PANEL]):
        rows = jnp.dot(pick.astype(bf16), part.astype(bf16), preferred_element_type=f32)
        top = rows if top is None else top + rows
    top = top * jnp.sum(pick * row_of(diag), axis=1, keepdims=True)
    position = jnp.sum(pick * iota((runs, PANEL), 1).astype(f32), axis=1, keepdims=True)
    within = jnp.sum(pick * (pivot_row % RUN).astype(f32), axis=1, keepdims=True)

    repeat(NY, lambda i: c_pass(i, True).wait_recv())

    first_row = (y * NC + c) * ROWS
    row_scale = jnp.sqrt(column_of(lanes_of(coulomb_ref, (y * NC + c) * 8, 8)))
    col_scale = jnp.sqrt(lanes_of(coulomb_ref, (x * NZ + z) * 4, 4))
    tile = 256

    def product(ref, rows, wanted):
        parts = []
        for j in wanted:
            zz = r_gather.z_at(j) if j else z
            for xx in range(2):
                owner = pl.multiple_of(owner_of(xx, zz) * OWN, OWN)
                parts.append(ref[xx, rows, pl.ds(owner, OWN)])
        return jnp.concatenate(parts, axis=1)

    done = [26, 26]
    groups = ((0, 1, 5, 2), (6, 3, 7), (4,))
    ready = {0: (21, 30, 31), 1: (20, 29, 31)}
    weights = aug[:, PANEL:] * pivot_scale_row
    everything = slice(None)
    for g, wanted in enumerate(groups):
        if g == len(groups) - 1:
            last_pivots = product(qp_ref, everything, wanted).astype(f32)
            direct = jnp.dot(weights, last_pivots, precision=HI, preferred_element_type=f32)
            for i, part in enumerate(split3(direct)):
                direct_ref[:, i * 2 * OWN : (i + 1) * 2 * OWN] = part.astype(bf16)
        for core in range(2):
            r_gather.run_core(core, done[core], ready[core][g] + 1)
            done[core] = max(done[core], ready[core][g] + 1)
        c_part = product(c_ref, everything, wanted)
        q_part = product(qp_ref, everything, wanted)
        for t in range(ROWS // tile):
            rows = slice(t * tile, (t + 1) * tile)
            scale = row_scale[rows]
            numbers = first_row + t * tile + iota((tile, COLS), 0)
            r_part = product(r_ref, rows, wanted)
            if g == 0:
                dielectric_ref[rows, :], panel_ref[rows, :] = times_t(r_part, c_part), times_t(r_part, q_part)
                continue
            gram = dielectric_ref[rows, :] + times_t(r_part, c_part)
            if g == 1:
                dielectric_ref[rows, :] = gram
                columns = panel_ref[rows, :] + times_t(r_part, q_part)
                same = numbers == pivot_row
                columns_ref[...] = scale * pivot_scale_row * columns + jnp.where(same, 1.0, 0.0)
                panel_ref[rows, :256] = times_t(columns_ref[:, :256], aug[:256, PANEL : PANEL + 256], HI)
                panel_ref[rows, 256:] = times_t(columns_ref[...], aug[256:, PANEL:], HI)
                continue
            same = numbers == first_col + iota((tile, COLS), 1)
            dielectric_ref[rows, :] = scale * col_scale * gram + jnp.where(same, 1.0, 0.0)
            three = jnp.concatenate([r_part] * 3, axis=1)
            panel_ref[rows, :] = panel_ref[rows, :] + scale * times_t(three, direct_ref[...])

    lane = iota((RUN, PANEL), 1).astype(f32)
    line = iota((RUN, PANEL), 0).astype(f32)
    for q in range(runs):
        rows = slice(q * RUN, (q + 1) * RUN)
        over = (line == within[q : q + 1]) & (lane >= position[q : q + 1])
        panel_ref[rows, :] = jnp.where(over, jnp.broadcast_to(top[q : q + 1, :], (RUN, PANEL)), panel_ref[rows, :])

    for d in range(1, NY):
        picked_copy(d).wait_send()

    @pl.when(jnp.logical_not(stays))
    def _():
        away.wait_send()

    @pl.when(jnp.logical_not(arrives))
    def _():
        onward.wait_send()

    for step in range(1, 5):
        for copy in c_copies(step, False):
            copy.wait_send()
    repeat(NY, lambda i: c_pass(i).wait_send())
    q_gather.drain()
    r_gather.drain()


def body(pair_density, pair_weight, coulomb, pivot_rows):
    vmem = pl.BlockSpec(memory_space=pltpu.VMEM)
    dma = pltpu.SemaphoreType.DMA
    return pl.pallas_call(
        main_kernel,
        out_shape=(
            jax.ShapeDtypeStruct((ROWS, COLS), f32),
            jax.ShapeDtypeStruct((ROWS, PANEL), f32),
        ),
        in_specs=[pl.BlockSpec(memory_space=pl.ANY)] * 4,
        out_specs=(vmem, vmem),
        scratch_shapes=[
            pltpu.VMEM((2, NX, NZ * MINE, HALF), bf16),
            pltpu.VMEM((2, ROWS, HALF), bf16),
            pltpu.VMEM((2, COLS, HALF), bf16),
            pltpu.VMEM((2, PANEL, HALF), bf16),
            pltpu.VMEM((PANEL, 2 * PANEL), f32),
            pltpu.VMEM((128, 256), f32),
            pltpu.VMEM((256, PANEL), f32),
            pltpu.VMEM((COLS, OWN), bf16),
            pltpu.VMEM((1, OWN), f32),
            pltpu.VMEM((128, 128), f32),
            pltpu.VMEM((4, 128), jnp.int32),
            pltpu.VMEM((COLS, OWN), bf16),
            pltpu.VMEM((MINE, OWN), bf16),
            pltpu.VMEM((COLS, OWN), bf16),
            pltpu.VMEM((PANEL, 6 * OWN), bf16),
            dma((4,)),
            dma((NY,)),
            dma((NY,)),
            dma((20,)),
            dma((20,)),
            dma((36,)),
            dma((36,)),
            dma((7,)),
            dma((7,)),
            dma((2,)),
            dma((2,)),
            dma((NZ,)),
            dma((NZ,)),
            dma((NY,)),
            dma((NY,)),
        ],
        compiler_params=pltpu.CompilerParams(
            collective_id=0, has_side_effects=True, vmem_limit_bytes=40 * 2**20
        ),
        name="gather_factor_panel",
    )(
        *(
            pltpu.with_memory_space_constraint(a, pltpu.HBM)
            for a in (pair_density, pair_weight.reshape(1, OWN), coulomb.reshape(128, 128), pivot_rows.reshape(4, 128))
        )
    )


def solution(mesh):
    finer = Mesh(mesh.devices.reshape(NY, NC, NX, NZ), ("y", "c", "x", "z"))
    return jax.shard_map(
        body,
        mesh=finer,
        in_specs=(P(("x", "z"), ("y", "c")), P(("y", "c")), P(), P()),
        out_specs=(P(("y", "c"), ("x", "z")), P(("y", "c"), None)),
        check_vma=False,
    )
```

```python
import functools

import jax
import jax.numpy as jnp
from jax import lax
from jax.experimental import pallas as pl
from jax.experimental.pallas import tpu as pltpu
from jax.sharding import Mesh
from jax.sharding import PartitionSpec as P

NG = 16384
PANEL = 512
RUN = NG // PANEL
NY, NC, NX, NZ = 8, 2, 4, 8
COLS = NG // (NX * NZ)
ROWS = NG // (NY * NC)
OWN = 128
HALF = NY * OWN
MINE = COLS // RUN
HI = lax.Precision.HIGHEST
f32, bf16 = jnp.float32, jnp.bfloat16
MESH_ID = pl.DeviceIdType.MESH


def iota(shape, dim):
    return lax.broadcasted_iota(jnp.int32, shape, dim)


def eye(n):
    return iota((n, n), 0) == iota((n, n), 1)


def column_of(row):
    blocks = []
    for i in range(row.shape[1] // 128):
        part = jnp.broadcast_to(row[:, i * 128 : (i + 1) * 128], (128, 128))
        blocks.append(jnp.sum(jnp.where(eye(128), part, 0.0), axis=1, keepdims=True))
    return jnp.concatenate(blocks, axis=0)


def row_of(column):
    blocks = []
    for i in range(column.shape[0] // 128):
        part = jnp.broadcast_to(column[i * 128 : (i + 1) * 128], (128, 128))
        blocks.append(jnp.sum(jnp.where(eye(128), part, 0.0), axis=0, keepdims=True))
    return jnp.concatenate(blocks, axis=1)


def lanes_of(ref, first, count):
    return jnp.concatenate([ref[pl.ds(first + i, 1), :] for i in range(count)], axis=1)


def times_t(a, b, precision=None):
    return lax.dot_general(
        a, b, (((1,), (1,)), ((), ())), precision=precision, preferred_element_type=f32
    )


def t_times(a, b, precision=None):
    return lax.dot_general(
        a, b, (((0,), (0,)), ((), ())), precision=precision, preferred_element_type=f32
    )


def split3(y):
    high = y.astype(bf16).astype(f32)
    rest = y - high
    middle = rest.astype(bf16).astype(f32)
    return high, middle, rest - middle


def eight_rows(s_ref, c):
    sub = iota((8, 128), 0)

    def taken(first):
        rows = s_ref[first : first + 8, :]
        cols = [jnp.broadcast_to(rows[:, c + j : c + j + 1], (8, 128)) for j in range(8)]
        return [cols, rows[:, :128], rows[:, 128:]]

    ahead = [first for first in (c + 8, c + 16) if first < 128]
    cols, left, right = taken(c)
    later = [taken(first) for first in ahead]
    for j in range(8):
        r = lax.rsqrt(jnp.broadcast_to(cols[j][j : j + 1, :], (8, 128)))
        f = jnp.where(sub > j, cols[j] * r, 0.0)
        own = jnp.where(sub == j, r, 1.0)
        factors = [part[0][j] * r for part in later]
        for m in range(j + 1, 8):
            pivot = jnp.broadcast_to(cols[m][j : j + 1, :], (8, 128)) * r
            cols[m] = cols[m] - f * pivot
            for part, g in zip(later, factors):
                part[0][m] = part[0][m] - g * pivot
        left_j = jnp.broadcast_to(left[j : j + 1, :], (8, 128)) * r
        right_j = jnp.broadcast_to(right[j : j + 1, :], (8, 128)) * r
        left = left * own - f * left_j
        right = right * own - f * right_j
        for part, g in zip(later, factors):
            part[1] = part[1] - g * left_j
            part[2] = part[2] - g * right_j
    y = jnp.concatenate([left, right], axis=1)
    s_ref[c : c + 8, :] = y
    for first, part in zip(ahead, later):
        s_ref[first : first + 8, :] = jnp.concatenate(part[1:], axis=1)
    rest = c + 24
    if rest < 128:
        h, m, l = split3(y)
        lhs = jnp.concatenate([h, h, m, h, l, m], axis=0)[:, :128].astype(bf16)
        rhs = jnp.concatenate([h, m, h, l, h, m], axis=0).astype(bf16)
        s_ref[rest:, :] = s_ref[rest:, :] - t_times(lhs, rhs)[rest:, :]


def factor_and_inverse(aug, s_ref, between):
    def block(k, carry):
        o = pl.multiple_of(k * 128, 128)
        span = pl.ds(o, PANEL + 128)
        s_ref[:, :128] = aug[pl.ds(o, 128), pl.ds(o, 128)]
        s_ref[:, 128:] = eye(128).astype(f32)
        for b in range(16):
            if b % 4 == 0:
                between(k, b // 4)
            eight_rows(s_ref, 8 * b)
        aug[pl.ds(o, 128), span] = jnp.dot(
            s_ref[:, 128:], aug[pl.ds(o, 128), span], precision=HI, preferred_element_type=f32
        )
        for i in range(1, 4):

            @pl.when(i > k)
            def _():
                lhs = aug[pl.ds(o, 128), i * 128 : (i + 1) * 128]
                update = t_times(lhs, aug[pl.ds(o, 128), span], HI)
                aug[i * 128 : (i + 1) * 128, span] = aug[i * 128 : (i + 1) * 128, span] - update

        return carry

    lax.fori_loop(0, 4, block, 0)


def pick_pivots(scaled, pivot_column, first):
    waves = (first + iota((PANEL, COLS), 1)).astype(f32)
    taken = jnp.sum(jnp.where(pivot_column == waves, 1.0, 0.0), axis=0, keepdims=True)
    in_run = iota((MINE, COLS), 1) // RUN == iota((MINE, COLS), 0)
    one_hot = jnp.where(in_run, jnp.broadcast_to(taken, (MINE, COLS)), 0.0).astype(bf16)
    return jnp.dot(one_hot, scaled, preferred_element_type=f32).astype(bf16)


class Gather:
    def __init__(self, sems, place):
        self.sems, self.place = sems, place
        y, c, x, z = place
        self.right_x, self.left_x = self.to_x(1), self.to_x(NX - 1)
        self.right_z, self.left_z = self.to_z(1), self.to_z(NZ - 1)

    def to_x(self, d):
        y, c, x, z = self.place
        return (y, c, lax.rem(x + d, NX), z)

    def to_z(self, d):
        y, c, x, z = self.place
        return (y, c, x, lax.rem(z + d, NZ))

    def z_at(self, j):
        z = self.place[3]
        return lax.rem(z + (NZ - j if j <= 4 else j - 4), NZ)

    def x_at(self, i):
        return lax.rem(self.place[2] + (0, NX - 1, 1, 2)[i], NX)

    def copy(self, ref, k, device):
        send, recv = self.sems
        return pltpu.make_async_remote_copy(ref, ref, send.at[k], recv.at[k], device, MESH_ID)

    def run(self, first, last=None):
        for core in range(2):

            @pl.when(self.place[1] == core)
            def _():
                self.process(self.events(core)[first : first + 1 if last is None else last])

    def process(self, events):
        for waits, sends, passes in events:
            for ref, k in waits:
                self.copy(ref, k, self.right_x).wait_recv()
            for ref, k, device in sends:
                self.copy(ref, k, device).start()
            for line in passes:
                self.line(*line).start()

    def run_core(self, core, first, last):
        if first < last:

            @pl.when(self.place[1] == core)
            def _():
                self.process(self.events(core)[first:last])

    def drain(self, first=0, last=None):
        for core in range(2):

            @pl.when(self.place[1] == core)
            def _():
                for waits, sends, passes in self.events(core)[first:last]:
                    for ref, k, device in sends:
                        self.copy(ref, k, device).wait_send()
                    for line in passes:
                        self.line(*line).wait_send()


class PivotGather(Gather):
    def __init__(self, q_ref, sems, pass_sems, place):
        super().__init__(sems, place)
        self.q_ref, self.pass_sems = q_ref, pass_sems

    def at(self, xs, z=None, core=None, rows=None):
        if z is not None:
            rows = pl.ds(pl.multiple_of(z * MINE, MINE), MINE)
        return self.q_ref.at[self.place[1] if core is None else core, xs, slice(None) if rows is None else rows, :]

    def passed(self, ref, k):
        send, recv = self.pass_sems
        y, c, x, z = self.place
        return pltpu.make_async_remote_copy(ref, ref, send.at[k], recv.at[k], (y, 1 - c, x, z), MESH_ID)

    def line(self, core, i, back=False):
        owner = 1 - self.place[1] if back else self.place[1]
        return self.passed(self.at(i, core=owner) if core == 0 else self.at(slice(None), i, core=owner), i)

    def wait_passed(self):
        for core in range(2):

            @pl.when(self.place[1] == core)
            def _():
                def step(i, carry):
                    self.line(1 - core, i, True).wait_recv()
                    return carry

                lax.fori_loop(0, NZ if core == 0 else NX, step, 0)

    def events(self, core):
        x, z = self.place[2:]
        everything = slice(None)
        if core == 0:
            start = [(self.at(x, z), d, self.to_z(d)) for d in (4, 3, 5, 2, 6, 1, 7)]
            arrive = [(self.at(x, lax.rem(z + NZ - d, NZ)), d) for d in range(1, NZ)]
            mine, a, b, o = (self.x_at(i) for i in range(4))
            whole = [(self.at(mine), 8, self.right_x), (self.at(mine), 9, self.left_x)]
            low, high = pl.ds(0, 64), pl.ds(64, 64)
            first = ([(self.at(a), 8)], [(self.at(a, rows=low), 10, self.right_x)], [(0, a)])
            second = ([(self.at(b), 9)], [(self.at(b, rows=high), 11, self.left_x)], [(0, b)])
            both = [(self.at(o, rows=low), 10), (self.at(o, rows=high), 11)]
            none = ([], [], [])
            return [([], start, []), none, none, (arrive, whole, [(0, mine)]), none, first, second, none, (both, [], [(0, o)])]

        def part(zz, m):
            return self.at(pl.ds(2 * m, 2), zz)

        def key(step, m, side):
            return 4 + 4 * (step - 1) + 2 * m + side

        def onward(step, zz, m):
            out = []
            if step < 4 or m == 0:
                out.append((part(zz[0], m), key(step, m, 0), self.right_z))
            if step < 4 or m == 1:
                out.append((part(zz[1], m), key(step, m, 1), self.left_z))
            return out

        start = [(self.at(x, z), d, self.to_x(d)) for d in (2, 1, 3)]
        arrive = [(self.at(lax.rem(x + NX - d, NX), z), d) for d in range(1, NX)]
        out = [([], start, []), (arrive, onward(1, (z, z), 0) + onward(1, (z, z), 1), [(1, z)])]
        for step in (1, 2, 3):
            zz = self.z_at(step), self.z_at(step + 4)
            for m in range(2):
                waits = [(part(zz[side], m), key(step, m, side)) for side in range(2)]
                out.append((waits, onward(step + 1, zz, m), [(1, zz[side]) for side in range(2)] if m else []))
        far = self.z_at(4)
        out.append(([(part(far, 0), key(4, 0, 0)), (part(far, 1), key(4, 1, 1))], [], [(1, far)]))
        return out


class RowGather(Gather):
    RIGHT = ((1, 0), (2, 0), (1, 1), (1, 2), (1, 3), (3, 0), (2, 1), (2, 2), (2, 3), (4, 0), (3, 1), (3, 2), (3, 3), (4, 1))
    LEFT = ((1, 0), (2, 0), (1, 1), (1, 2), (1, 3), (3, 0), (2, 1), (2, 2), (2, 3), (3, 1), (3, 2), (4, 2), (3, 3), (4, 3))

    def __init__(self, slot, sems, place):
        super().__init__(sems, place)
        self.slot = slot

    def events(self, core):
        x, z = self.place[2:]
        slot = self.slot
        out = []
        if core == 0:
            own = [(slot(x, z), 1, self.right_z), (slot(x, z), 5, self.left_z)]
            own += [(slot(x, z), 8, self.right_x), (slot(x, z), 16, self.left_x)]
            out.append(([], own, []))
            order = (0, 1, 5, 2, 6, 3, 7, 4)

            def along_z(j):
                here = slot(x, self.z_at(j))
                waits, sends = [(here, j)], []
                if j == 4:
                    waits = [(slot(x, self.z_at(4), 0), 4), (slot(x, self.z_at(4), 1), 32)]
                elif j == 3:
                    sends = [(slot(x, self.z_at(3), 0), 4, self.right_z)]
                elif j == 7:
                    sends = [(slot(x, self.z_at(7), 1), 32, self.left_z)]
                else:
                    sends = [(here, j + 1, self.right_z if j < 4 else self.left_z)]
                return waits, sends + [(here, 8 + j, self.right_x), (here, 16 + j, self.left_x)], []

            def along_x(p, side):
                j = order[p]
                here = slot(self.x_at(1 + side), self.z_at(j) if j else z)
                sends = [(here, 24 + j, self.left_x if side else self.right_x)] if p % 2 == side else []
                return [(here, (16 if side else 8) + j)], sends, []

            def opposite(p):
                j = order[p]
                return [(slot(self.x_at(3), self.z_at(j) if j else z), 24 + j)], [], []

            out += [along_z(1), along_z(5), along_x(0, 0), along_x(0, 1), along_z(2), along_z(6)]
            out += [along_x(1, 0), along_x(1, 1), opposite(0), along_z(3), along_z(7)]
            out += [along_x(2, 0), along_x(2, 1), opposite(1), along_z(4)]
            for p in range(3, 8):
                out += [along_x(p, 0), along_x(p, 1), opposite(p - 1)]
            out.append(opposite(7))
            return out

        def key(step, i, side):
            return 4 + 8 * (step - 1) + 2 * i + side

        def onward(step, i, side, here):
            if step > 4 or (step == 4 and i // 2 != side):
                return []
            return [(here, key(step, i, side), self.left_z if side else self.right_z)]

        def along(step, i, side):
            here = slot(self.x_at(i), self.z_at(step + 4 * side if step < 4 else 4))
            return [(here, key(step, i, side))], onward(step + 1, i, side, here), []

        own = [(slot(x, z), d, self.to_x(d)) for d in (2, 1, 3)]
        out.append(([], own + onward(1, 0, 0, slot(x, z)) + onward(1, 0, 1, slot(x, z)), []))
        right, left = list(self.RIGHT), list(self.LEFT)
        out += [along(*right.pop(0), 0), along(*left.pop(0), 1)]
        for i, d in ((1, 1), (2, 3), (3, 2)):
            here = slot(self.x_at(i), z)
            out.append(([(here, d)], onward(1, i, 0, here) + onward(1, i, 1, here), []))
        while right:
            out += [along(*right.pop(0), 0), along(*left.pop(0), 1)]
        return out


EVENTS = 32


def main_kernel(
    density_in,
    weight_in,
    coulomb_in,
    pivots_in,
    dielectric_ref,
    panel_ref,
    q_ref,
    r_ref,
    c_ref,
    qp_ref,
    aug,
    s_ref,
    columns_ref,
    density_ref,
    weight_ref,
    coulomb_ref,
    pivots_ref,
    scaled_ref,
    picked_ref,
    mid_ref,
    direct_ref,
    local_sem,
    qy_send,
    qy_recv,
    qg_send,
    qg_recv,
    rg_send,
    rg_recv,
    cy_send,
    cy_recv,
    one_send,
    one_recv,
    qx_send,
    qx_recv,
    cx_send,
    cx_recv,
):
    y, c, x, z = (lax.axis_index(a) for a in ("y", "c", "x", "z"))
    place = (y, c, x, z)
    partner = (y, 1 - c, x, z)

    to_y, to_c = 2 * x + z // 4, lax.rem(z // 2, 2)
    mid_x, mid_z = 2 * lax.rem(z, 2) + c, lax.rem(y + 4 * c + 8 - to_y + 4 * (z // 4) + 2 * to_c, NZ)
    middle = (y, to_c, mid_x, mid_z)
    stays = (mid_x == x) & (mid_z == z) & (to_c == c)

    turn = lax.rem(y + 4 * lax.rem(x, 2) + 2 * c + 8 - z, NZ)
    odd = lax.rem(turn, 2)
    origin = (y, lax.rem(x, 2), lax.rem(turn + 3 * odd, 8) // 2, 4 * odd + 2 * c + x // 2)
    last_y = lax.rem(turn + 4 * odd, NY)
    arrives = last_y == y

    def owner_of(xx, zz):
        return lax.rem(zz + y + 16 - 4 * lax.rem(y, 2) - 2 * c + 4 * lax.rem(xx, 2), NY)

    def r_block(pair_core, half, owner):
        return r_ref.at[
            pair_core,
            pl.ds(pl.multiple_of(half * COLS, COLS), COLS),
            pl.ds(pl.multiple_of(owner * OWN, OWN), OWN),
        ]

    def r_slot(xx, zz, part=None):
        first, count = (xx // 2) * COLS, COLS
        if part is not None:
            first, count = first + part * (COLS // 2), COLS // 2
        return r_ref.at[
            lax.rem(xx, 2),
            pl.ds(pl.multiple_of(first, 256), count),
            pl.ds(pl.multiple_of(owner_of(xx, zz) * OWN, OWN), OWN),
        ]

    q_gather = PivotGather(q_ref, (qg_send, qg_recv), (qx_send, qx_recv), place)
    r_gather = RowGather(r_slot, (rg_send, rg_recv), place)

    barrier = pltpu.get_barrier_semaphore()
    greeted = [middle, origin]
    greeted += [(lax.rem(y + d, NY), c, x, z) for d in (4, 3, 5, 2, 6, 1, 7)]
    greeted += [(y, c, x, lax.rem(z + d, NZ)) for d in range(1, NZ)]
    greeted += [(y, c, lax.rem(x + d, NX), z) for d in range(1, NX)]
    greeted += [partner]
    for device in greeted:
        pl.semaphore_signal(barrier, 1, device_id=device, device_id_type=MESH_ID)

    inputs = [
        pltpu.make_async_copy(density_in, density_ref, local_sem.at[0]),
        pltpu.make_async_copy(weight_in, weight_ref, local_sem.at[1]),
        pltpu.make_async_copy(pivots_in, pivots_ref, local_sem.at[2]),
        pltpu.make_async_copy(coulomb_in, coulomb_ref, local_sem.at[3]),
    ]
    for copy in inputs:
        copy.start()
    for copy in inputs:
        copy.wait()
    pivot_row = jnp.concatenate([pivots_ref[i : i + 1, :] for i in range(4)], axis=1)
    first_col = (x * NZ + z) * COLS
    scaled = (density_ref[...].astype(f32) * jnp.sqrt(weight_ref[...])).astype(bf16)
    picked_own = pick_pivots(scaled, column_of(pivot_row.astype(f32)), first_col)
    own_rows = pl.ds(pl.multiple_of(z * MINE, MINE), MINE)
    own_pairs = pl.ds(pl.multiple_of(y * OWN, OWN), OWN)
    scaled_ref[...] = scaled
    picked_ref[...] = picked_own
    c_ref[c, :, own_pairs] = scaled
    q_ref[c, x, own_rows, own_pairs] = picked_own
    own_q = q_ref.at[c, x, own_rows, own_pairs]
    pl.semaphore_wait(barrier, len(greeted))

    def picked_copy(d):
        peer = (lax.rem(y + d, NY), c, x, z)
        return pltpu.make_async_remote_copy(
            picked_ref, own_q, qy_send.at[d], qy_recv.at[d], peer, MESH_ID
        )

    def picked_arrival(d):
        other = lax.rem(y + NY - d, NY)
        there = q_ref.at[c, x, own_rows, pl.ds(pl.multiple_of(other * OWN, OWN), OWN)]
        return pltpu.make_async_remote_copy(
            there, there, qy_send.at[d], qy_recv.at[d], partner, MESH_ID
        )

    for d in (4, 3, 5, 2, 6, 1, 7):
        picked_copy(d).start()

    away = pltpu.make_async_remote_copy(scaled_ref, mid_ref, one_send.at[0], one_recv.at[0], middle, MESH_ID)
    stay = pltpu.make_async_copy(scaled_ref, mid_ref, local_sem.at[0])
    here = r_slot(x, z)
    there = r_block(lax.rem(x, 2), x // 2, y)
    onward = pltpu.make_async_remote_copy(mid_ref, there, one_send.at[1], one_recv.at[1], (last_y, c, x, z), MESH_ID)
    onward_in = pltpu.make_async_remote_copy(here, here, one_send.at[1], one_recv.at[1], partner, MESH_ID)
    keep = pltpu.make_async_copy(mid_ref, here, local_sem.at[1])

    def either(condition, yes, no):
        pl.when(condition)(yes)
        pl.when(jnp.logical_not(condition))(no)

    def second_move():
        either(stays, stay.wait, away.wait_recv)
        either(arrives, keep.start, onward.start)

    def c_of(owner):
        return c_ref.at[c, :, pl.ds(pl.multiple_of(owner * OWN, OWN), OWN)]

    def ring_y(step):
        up, down = (lax.rem(y + 1, NY), c, x, z), (lax.rem(y + NY - 1, NY), c, x, z)
        k = 2 * (step - 1)
        out = [(c_of(lax.rem(y + NY - step + 1, NY)), c_of(lax.rem(y + NY - step, NY)), k, up)]
        if step < 4:
            out.append((c_of(lax.rem(y + step - 1, NY)), c_of(lax.rem(y + step, NY)), k + 1, down))
        return out

    def c_copies(step, received):
        for sent, came, k, device in ring_y(step):
            ref = came if received else sent
            yield pltpu.make_async_remote_copy(ref, ref, cy_send.at[k], cy_recv.at[k], device, MESH_ID)

    def c_pass(owner, back=False):
        ref = c_ref.at[1 - c if back else c, :, pl.ds(pl.multiple_of(owner * OWN, OWN), OWN)]
        return pltpu.make_async_remote_copy(ref, ref, cx_send.at[owner], cx_recv.at[owner], partner, MESH_ID)

    def c_advance(event):
        if event > 1:
            for copy in c_copies(event - 1, True):
                copy.wait_recv()
            for away in (NY - event + 1, event - 1)[: 2 if event < 5 else 1]:
                c_pass(lax.rem(y + away, NY)).start()
        if event < 5:
            for copy in c_copies(event, False):
                copy.start()

    def repeat(count, do):
        def step(i, carry):
            do(i)
            return carry

        lax.fori_loop(0, count, step, 0)

    either(stays, stay.start, away.start)
    run_column = column_of((pivot_row // RUN).astype(f32))
    high_column = column_of((pivot_row // 128).astype(f32))
    low_column = column_of((pivot_row % 128).astype(f32))
    in_row = (high_column == iota((PANEL, 128), 1).astype(f32)).astype(f32)
    picked = jnp.dot(in_row, coulomb_ref[...], precision=HI, preferred_element_type=f32)
    at_lane = low_column == iota((PANEL, 128), 1).astype(f32)
    pivot_scale = jnp.sqrt(jnp.sum(jnp.where(at_lane, picked, 0.0), axis=1, keepdims=True))
    pivot_scale_row = row_of(pivot_scale)
    order = (run_column == iota((PANEL, PANEL), 1).astype(f32)).astype(bf16)

    for d in range(1, NY):
        picked_arrival(d).wait_recv()
    q_gather.run(0, 2)
    second_move()
    c_pass(y).start()
    c_advance(1)
    q_gather.run(2, 4)
    either(arrives, keep.wait, onward_in.wait_recv)
    r_gather.run(0)
    q_gather.run(4)
    q_gather.run(5, 7)
    c_advance(2)
    r_gather.run(1, 3)
    q_gather.run(7, 9)
    q_gather.wait_passed()

    gram = None
    for h in range(2):
        qp_ref[h] = jnp.dot(
            order, q_ref[h].reshape(PANEL, HALF), preferred_element_type=f32
        ).astype(bf16)
        part = times_t(qp_ref[h], qp_ref[h])
        gram = part if gram is None else gram + part
    unit = eye(PANEL).astype(f32)
    aug[:, :PANEL] = pivot_scale * pivot_scale_row * gram + unit
    aug[:, PANEL:] = unit
    r_gather.run(3, 7)
    c_advance(3)

    def between(k, part):
        for block in range(4):
            at = 4 * block + part
            low, high = (7 + (19 * i) // 16 for i in (at, at + 1))
            if low < high or at in (4, 8):

                @pl.when(k == block)
                def _():
                    r_gather.run(low, high)
                    if at == 4:
                        c_advance(4)
                    if at == 8:
                        c_advance(5)

    factor_and_inverse(aug, s_ref, between)

    diag = jnp.concatenate(
        [
            jnp.sum(jnp.where(eye(128), aug[i : i + 128, i : i + 128], 0.0), axis=1, keepdims=True)
            for i in range(0, PANEL, 128)
        ],
        axis=0,
    )
    aug[:, PANEL:] = aug[:, PANEL:] / diag

    runs = ROWS // RUN
    run_row = pivot_row // RUN
    pick = (run_row == (y * NC + c) * runs + iota((runs, PANEL), 0)).astype(f32)
    top = None
    for part in split3(aug[:, :PANEL]):
        rows = jnp.dot(pick.astype(bf16), part.astype(bf16), preferred_element_type=f32)
        top = rows if top is None else top + rows
    top = top * jnp.sum(pick * row_of(diag), axis=1, keepdims=True)
    position = jnp.sum(pick * iota((runs, PANEL), 1).astype(f32), axis=1, keepdims=True)
    within = jnp.sum(pick * (pivot_row % RUN).astype(f32), axis=1, keepdims=True)

    repeat(NY, lambda i: c_pass(i, True).wait_recv())

    first_row = (y * NC + c) * ROWS
    row_scale = jnp.sqrt(column_of(lanes_of(coulomb_ref, (y * NC + c) * 8, 8)))
    col_scale = jnp.sqrt(lanes_of(coulomb_ref, (x * NZ + z) * 4, 4))
    tile = 256

    def product(ref, rows, wanted):
        parts = []
        for j in wanted:
            zz = r_gather.z_at(j) if j else z
            for xx in range(2):
                owner = pl.multiple_of(owner_of(xx, zz) * OWN, OWN)
                parts.append(ref[xx, rows, pl.ds(owner, OWN)])
        return jnp.concatenate(parts, axis=1)

    for d in range(1, NY):
        picked_copy(d).wait_send()

    @pl.when(jnp.logical_not(stays))
    def _():
        away.wait_send()

    @pl.when(jnp.logical_not(arrives))
    def _():
        onward.wait_send()

    for step in range(1, 5):
        for copy in c_copies(step, False):
            copy.wait_send()
    repeat(NY, lambda i: c_pass(i).wait_send())
    q_gather.drain()
    r_gather.drain(0, 20)

    done = [26, 26]
    groups = ((0, 1, 5, 2), (6, 3, 7), (4,))
    ready = {0: (21, 30, 31), 1: (20, 29, 31)}
    weights = aug[:, PANEL:] * pivot_scale_row
    everything = slice(None)
    for g, wanted in enumerate(groups):
        if g == len(groups) - 1:
            last_pivots = product(qp_ref, everything, wanted).astype(f32)
            direct = jnp.dot(weights, last_pivots, precision=HI, preferred_element_type=f32)
            for i, part in enumerate(split3(direct)):
                direct_ref[:, i * 2 * OWN : (i + 1) * 2 * OWN] = part.astype(bf16)
        for core in range(2):
            r_gather.run_core(core, done[core], ready[core][g] + 1)
            done[core] = max(done[core], ready[core][g] + 1)
        c_part = product(c_ref, everything, wanted)
        q_part = product(qp_ref, everything, wanted)
        for t in range(ROWS // tile):
            rows = slice(t * tile, (t + 1) * tile)
            scale = row_scale[rows]
            numbers = first_row + t * tile + iota((tile, COLS), 0)
            r_part = product(r_ref, rows, wanted)
            if g == 0:
                dielectric_ref[rows, :], panel_ref[rows, :] = times_t(r_part, c_part), times_t(r_part, q_part)
                continue
            gram = dielectric_ref[rows, :] + times_t(r_part, c_part)
            if g == 1:
                dielectric_ref[rows, :] = gram
                columns = panel_ref[rows, :] + times_t(r_part, q_part)
                same = numbers == pivot_row
                columns_ref[...] = scale * pivot_scale_row * columns + jnp.where(same, 1.0, 0.0)
                panel_ref[rows, :256] = times_t(columns_ref[:, :256], aug[:256, PANEL : PANEL + 256], HI)
                panel_ref[rows, 256:] = times_t(columns_ref[...], aug[256:, PANEL:], HI)
                continue
            same = numbers == first_col + iota((tile, COLS), 1)
            dielectric_ref[rows, :] = scale * col_scale * gram + jnp.where(same, 1.0, 0.0)
            three = jnp.concatenate([r_part] * 3, axis=1)
            panel_ref[rows, :] = panel_ref[rows, :] + scale * times_t(three, direct_ref[...])

    lane = iota((RUN, PANEL), 1).astype(f32)
    line = iota((RUN, PANEL), 0).astype(f32)
    for q in range(runs):
        rows = slice(q * RUN, (q + 1) * RUN)
        over = (line == within[q : q + 1]) & (lane >= position[q : q + 1])
        panel_ref[rows, :] = jnp.where(over, jnp.broadcast_to(top[q : q + 1, :], (RUN, PANEL)), panel_ref[rows, :])

    r_gather.drain(20)


def body(pair_density, pair_weight, coulomb, pivot_rows):
    vmem = pl.BlockSpec(memory_space=pltpu.VMEM)
    dma = pltpu.SemaphoreType.DMA
    return pl.pallas_call(
        main_kernel,
        out_shape=(
            jax.ShapeDtypeStruct((ROWS, COLS), f32),
            jax.ShapeDtypeStruct((ROWS, PANEL), f32),
        ),
        in_specs=[pl.BlockSpec(memory_space=pl.ANY)] * 4,
        out_specs=(vmem, vmem),
        scratch_shapes=[
            pltpu.VMEM((2, NX, NZ * MINE, HALF), bf16),
            pltpu.VMEM((2, ROWS, HALF), bf16),
            pltpu.VMEM((2, COLS, HALF), bf16),
            pltpu.VMEM((2, PANEL, HALF), bf16),
            pltpu.VMEM((PANEL, 2 * PANEL), f32),
            pltpu.VMEM((128, 256), f32),
            pltpu.VMEM((256, PANEL), f32),
            pltpu.VMEM((COLS, OWN), bf16),
            pltpu.VMEM((1, OWN), f32),
            pltpu.VMEM((128, 128), f32),
            pltpu.VMEM((4, 128), jnp.int32),
            pltpu.VMEM((COLS, OWN), bf16),
            pltpu.VMEM((MINE, OWN), bf16),
            pltpu.VMEM((COLS, OWN), bf16),
            pltpu.VMEM((PANEL, 6 * OWN), bf16),
            dma((4,)),
            dma((NY,)),
            dma((NY,)),
            dma((20,)),
            dma((20,)),
            dma((36,)),
            dma((36,)),
            dma((7,)),
            dma((7,)),
            dma((2,)),
            dma((2,)),
            dma((NZ,)),
            dma((NZ,)),
            dma((NY,)),
            dma((NY,)),
        ],
        compiler_params=pltpu.CompilerParams(
            collective_id=0, has_side_effects=True, vmem_limit_bytes=40 * 2**20
        ),
        name="gather_factor_panel",
    )(
        *(
            pltpu.with_memory_space_constraint(a, pltpu.HBM)
            for a in (pair_density, pair_weight.reshape(1, OWN), coulomb.reshape(128, 128), pivot_rows.reshape(4, 128))
        )
    )


def solution(mesh):
    finer = Mesh(mesh.devices.reshape(NY, NC, NX, NZ), ("y", "c", "x", "z"))
    return jax.shard_map(
        body,
        mesh=finer,
        in_specs=(P(("x", "z"), ("y", "c")), P(("y", "c")), P(), P()),
        out_specs=(P(("y", "c"), ("x", "z")), P(("y", "c"), None)),
        check_vma=False,
    )
```
